32 devices in a mesh: fsdp: 16 (over z, x, core), tp: 2 (over y).
Axes of the slice: x: 2, y: 2, z: 4, core: 2. Of those that a mesh axis runs over, the one named last changes fastest.
Arguments:
- tokens: bfloat16 [50176, 512], P(('fsdp', 'tp')), may hold values from -60 to 60
- cotangent: bfloat16 [50176, 512], P(('fsdp', 'tp')), may hold values from -6 to 6
- norm_gain: float32 [2, 2, 512], replicated, may hold values from 0.5 to 1.5
- norm_shift: float32 [2, 2, 512], replicated, may hold values from -3 to 3
- input_weight: bfloat16 [2, 3, 512, 512], P(None, None, 'fsdp', 'tp'), may hold values from -0.25 to 0.25
- head_bias: float32 [2, 2, 512], replicated, may hold values from -3 to 3
- offset_table: float32 [2, 169, 16], replicated, may hold values from -10 to 470
- output_weight: bfloat16 [2, 512, 512], P(None, 'tp', 'fsdp'), may hold values from -0.75 to 0.75
- output_bias: float32 [2, 512], replicated, may hold values from -3 to 3
- expand_weight: bfloat16 [2, 512, 2048], P(None, 'fsdp', 'tp'), may hold values from -0.25 to 0.25
- expand_bias: float32 [2, 2048], replicated, may hold values from -3 to 3
- reduce_weight: bfloat16 [2, 2048, 512], P(None, 'tp', 'fsdp'), may hold values from -0.125 to 0.125
- reduce_bias: float32 [2, 512], replicated, may hold values from -3 to 3
- offset_index: int32 [49, 49], replicated, may hold values from 0 to 168, as said below
- region_label: int32 [196], replicated, may hold values from 0 to 8, as said below
- roll_order: int32 [196], replicated, may hold values from 0 to 195, as said below
Outputs:
- outputs: bfloat16 [50176, 512], P(('fsdp', 'tp'))
- tokens_grad: bfloat16 [50176, 512], P(('fsdp', 'tp'))
- norm_gain_grad: float32 [2, 2, 512], replicated
- norm_shift_grad: float32 [2, 2, 512], replicated
- input_weight_grad: float32 [2, 3, 512, 512], P(None, None, 'fsdp', 'tp')
- head_bias_grad: float32 [2, 2, 512], replicated
- offset_table_grad: float32 [2, 169, 16], replicated
- output_weight_grad: float32 [2, 512, 512], P(None, 'tp', 'fsdp')
- output_bias_grad: float32 [2, 512], replicated
- expand_weight_grad: float32 [2, 512, 2048], P(None, 'fsdp', 'tp')
- expand_bias_grad: float32 [2, 2048], replicated
- reduce_weight_grad: float32 [2, 2048, 512], P(None, 'tp', 'fsdp')
- reduce_bias_grad: float32 [2, 512], replicated
The draws below stay inside these ranges and needn't reach their ends.
Inputs may be any that keep to these rules, and one draw needn't show every extreme that they name: `offset_index`: entry (i, j), with i = 7 a + b and j = 7 e + f, depends only on the offset (a - e, b - f); distinct offsets give distinct entries. `region_label`: the label of cell (row, column) is 3 r + s, where r is 0, 1 or 2 as the row lies in [0, 7), [7, 14 - sy) or [14 - sy, 14), and s likewise for the column with sx; the shifts sy and sx lie in 1 to 6. `roll_order`: position p = 49 ((2) u + v) + 7 a + b holds cell (((7 u + a + sy) mod 14) * 14 + (7 v + b + sx) mod 14), with the same shifts sy and sx as region_label; every cell appears once.
All inputs are finite; a program needn't handle non-finite values.
Results may differ from the reference program's by a relative error of at most 0.025.
Values may be sent and summed in bfloat16 or wider, within the bound.
No kernel may reach another device: no remote copies, remote signals or barrier semaphores. Data moves between devices by JAX's collectives and lax.ppermute only.
A program may use at most 384 MiB of HBM per device.

```python
import jax
import jax.numpy as jnp
from jax import lax

C = 512
HEADS = 16
HD = 32
HID = 2048
WIN = 7
RES = 14
LAYERS = 2
IMG_DEV = 16
WTOK = 49
NREL = 169
TOKENS = 50176
N_FSDP = 16
N_TP = 2


def roll_shift(key):
    return jax.random.randint(jax.random.fold_in(key, 5), (2,), 1, WIN)


def draw_tokens(key, part):
    row_key, col_key, base_key = jax.random.split(jax.random.fold_in(key, 3), 3)
    col_scale = jnp.exp(jax.random.uniform(col_key, (1, C), jnp.float32, -1.2, 1.2))
    row_scale = jnp.exp(jax.random.uniform(row_key, (TOKENS, 1), jnp.float32, -0.7, 0.7))
    base = jax.random.normal(base_key, (TOKENS, C), jnp.float32)
    return (base * col_scale * row_scale).astype(jnp.bfloat16)


def draw_offset_table(key, part):
    noise_key = jax.random.fold_in(jax.random.fold_in(key, 9), 0)
    noise = jnp.clip(jax.random.normal(noise_key, (LAYERS, NREL, HEADS), jnp.float32), -8.0, 8.0)
    return noise


def draw_offset_index(key, part):
    relabel = jax.random.permutation(jax.random.fold_in(key, 11), NREL)
    places = jnp.arange(WTOK, dtype=jnp.int32)
    row_part = places // WIN
    col_part = places % WIN
    standard = (row_part[:, None] - row_part[None, :] + WIN - 1) * (2 * WIN - 1) + (col_part[:, None] - col_part[None, :] + WIN - 1)
    return relabel[standard].astype(jnp.int32)


def draw_region_label(key, part):
    shift = roll_shift(key)
    cells = jnp.arange(RES, dtype=jnp.int32)
    band_row = (cells >= RES - WIN).astype(jnp.int32) + (cells >= RES - shift[0]).astype(jnp.int32)
    band_col = (cells >= RES - WIN).astype(jnp.int32) + (cells >= RES - shift[1]).astype(jnp.int32)
    return (3 * band_row[:, None] + band_col[None, :]).reshape(RES * RES).astype(jnp.int32)


def draw_roll_order(key, part):
    shift = roll_shift(key)
    places = jnp.arange(RES * RES, dtype=jnp.int32)
    window = places // WTOK
    inside = places % WTOK
    per_row = RES // WIN
    row_cell = (WIN * (window // per_row) + inside // WIN + shift[0]) % RES
    col_cell = (WIN * (window % per_row) + inside % WIN + shift[1]) % RES
    return (row_cell * RES + col_cell).astype(jnp.int32)


def spiked(drawn, stream_key, source, target, shards_of, factor):
    def block_of(axis_at):
        return (jnp.arange(drawn.shape[axis_at]) // (drawn.shape[axis_at] // shards_of)).reshape((-1,) + (1,) * (drawn.ndim - 1 - axis_at))

    first = jax.random.permutation(stream_key, shards_of)[block_of(target)]
    far = (block_of(target) + shards_of // 2) % shards_of
    return jnp.where((block_of(source) == first) | (block_of(source) == far), factor * drawn, drawn)


def block_scale(key, extent, pieces, low, high):
    level = 1.0
    for dim, shards_of in pieces:
        heights = jax.random.uniform(jax.random.fold_in(jax.random.fold_in(key, 6), dim), (shards_of,), jnp.float32, low / len(pieces), high / len(pieces))
        level = level * jnp.repeat(jnp.exp(heights), extent[dim] // shards_of).reshape((-1,) + (1,) * (len(extent) - 1 - dim))
    return level


def normal_values(rng, shape, spread, limit, cuts=(), kind=jnp.bfloat16):
    loudness = block_scale(rng, shape, cuts, -0.22, 0.18) if cuts else 1.0
    entries = jax.random.normal(rng, shape, jnp.float32) * spread * loudness
    return jnp.minimum(jnp.maximum(entries, -limit), limit).astype(kind)


def gaussian_with(rng, extent, scale, limit, cuts, heavy, kind=jnp.bfloat16):
    entries = scale * jax.random.normal(rng, extent, jnp.float32)
    if cuts:
        entries = entries * block_scale(rng, extent, cuts, -0.22, 0.18)
    return jnp.clip(spiked(entries, jax.random.fold_in(rng, 3), *heavy), -limit, limit).astype(kind)


def setup_inputs(seed: int = 0) -> dict:
    arg_keys = jax.random.split(jax.random.key(seed), 17)
    return {
        "tokens": draw_tokens(jax.random.fold_in(arg_keys[16], 71), 0),
        "cotangent": gaussian_with(arg_keys[1], (TOKENS, C), 1.0, 6.0, ((0, 32),), (0, 1, 32, 2.75)),
        "norm_gain": jnp.clip(1.0 + 0.1 * jax.random.normal(arg_keys[2], (LAYERS, 2, C), jnp.float32), 0.5, 1.5),
        "norm_shift": normal_values(arg_keys[3], (LAYERS, 2, C), 0.5, 3.0, (), jnp.float32),
        "input_weight": normal_values(arg_keys[4], (LAYERS, 3, C, C), C ** -0.5, 0.25, ((2, 16), (3, 2))),
        "head_bias": normal_values(arg_keys[5], (LAYERS, 2, C), 0.5, 3.0, (), jnp.float32),
        "offset_table": draw_offset_table(jax.random.fold_in(arg_keys[16], 71), 0),
        "output_weight": normal_values(arg_keys[7], (LAYERS, C, C), (C // WIN) ** -0.5, 0.75, ((1, 2), (2, 16))),
        "output_bias": normal_values(arg_keys[8], (LAYERS, C), 0.5, 3.0, (), jnp.float32),
        "expand_weight": normal_values(arg_keys[9], (LAYERS, C, HID), C ** -0.5, 0.25, ((1, 16), (2, 2))),
        "expand_bias": normal_values(arg_keys[10], (LAYERS, HID), 0.5, 3.0, (), jnp.float32),
        "reduce_weight": normal_values(arg_keys[11], (LAYERS, HID, C), HID ** -0.5, 0.125, ((1, 2), (2, 16))),
        "reduce_bias": normal_values(arg_keys[12], (LAYERS, C), 0.5, 3.0, (), jnp.float32),
        "offset_index": draw_offset_index(jax.random.fold_in(arg_keys[16], 71), 0),
        "region_label": draw_region_label(jax.random.fold_in(arg_keys[16], 71), 0),
        "roll_order": draw_roll_order(jax.random.fold_in(arg_keys[16], 71), 0),
    }


EPS = 1e-05
MASKED = -100.0

def matmul(operand, matrix):
    return jnp.dot(operand, matrix, preferred_element_type=jnp.float32)

def rounded(values):
    return lax.optimization_barrier(values.astype(jnp.bfloat16)).astype(jnp.float32)

def to_windows(token_rows, images, order, shifted):
    width = token_rows.shape[-1]
    if shifted:
        grid = token_rows.reshape(images, RES * RES, width)
        return jnp.take(grid, order, axis=1).reshape(images * RES * RES, width)
    blocks = RES // WIN
    grid = token_rows.reshape(images, blocks, WIN, blocks, WIN, width)
    return grid.transpose(0, 1, 3, 2, 4, 5).reshape(images * RES * RES, width)

def from_windows(window_rows, images, inverse, shifted):
    width = window_rows.shape[-1]
    if shifted:
        grid = window_rows.reshape(images, RES * RES, width)
        return jnp.take(grid, inverse, axis=1).reshape(images * RES * RES, width)
    blocks = RES // WIN
    grid = window_rows.reshape(images, blocks, blocks, WIN, WIN, width)
    return grid.transpose(0, 1, 3, 2, 4, 5).reshape(images * RES * RES, width)

def window_mask(region_label):
    blocks = RES // WIN
    labels = region_label.reshape(blocks, WIN, blocks, WIN).transpose(0, 2, 1, 3).reshape(blocks * blocks, WIN * WIN)
    same_region = labels[:, :, None] == labels[:, None, :]
    return jnp.where(same_region, jnp.float32(0.0), jnp.float32(MASKED))

def normalize(values, gain, shift):
    center = lax.optimization_barrier(jnp.mean(values, axis=-1, keepdims=True))
    centred = values - center
    inverse_scale = lax.rsqrt(lax.optimization_barrier(jnp.mean(centred * centred, axis=-1, keepdims=True)) + EPS)
    unit_rows = centred * inverse_scale
    return (unit_rows * gain + shift, unit_rows, inverse_scale)

def normalize_back(grad_normed, unit_rows, inverse_scale, gain):
    scaled = grad_normed * gain
    return inverse_scale * (scaled - lax.optimization_barrier(jnp.mean(scaled, axis=-1, keepdims=True)) - unit_rows * lax.optimization_barrier(jnp.mean(scaled * unit_rows, axis=-1, keepdims=True)))

def gelu_parts(before):
    normal_cdf = 0.5 * (1.0 + lax.erf(before * 0.7071067811865476))
    density = jnp.exp(-0.5 * before * before) * 0.3989422804014327
    return (before * normal_cdf, normal_cdf + before * density)

def scores_of(query_rows, key_rows, offset_bias, region_mask, shifted, images):
    pairs = WIN * WIN
    windows = query_rows.shape[0] // pairs
    head_count = query_rows.shape[1] // HD
    query_heads = query_rows.astype(jnp.float32).reshape(windows, pairs, head_count, HD)
    key_heads = key_rows.astype(jnp.float32).reshape(windows, pairs, head_count, HD)
    scores = jnp.einsum('wihd,wjhd->whij', query_heads, key_heads) + offset_bias[None]
    if shifted:
        blocks = (RES // WIN) ** 2
        scores = (scores.reshape(images, blocks, head_count, pairs, pairs) + region_mask[None, :, None]).reshape(windows, head_count, pairs, pairs)
    return scores

def split_sum(operands, matrices):
    width = operands[0].shape[1] // N_TP
    total = jnp.zeros((operands[0].shape[0], matrices[0].shape[1]), jnp.float32)
    for group_index in range(N_TP):
        partial_sum = jnp.zeros_like(total)
        for operand, matrix in zip(operands, matrices):
            partial_sum = partial_sum + matmul(operand[:, group_index * width:(group_index + 1) * width], matrix[group_index * width:(group_index + 1) * width])
        total = total + rounded(partial_sum)
    return total

def reference(tokens, cotangent, norm_gain, norm_shift, input_weight, head_bias, offset_table, output_weight, output_bias, expand_weight, expand_bias, reduce_weight, reduce_bias, offset_index, region_label, roll_order):
    images = IMG_DEV
    group_rows = images * RES * RES
    pairs = WIN * WIN
    windows = group_rows // pairs
    scale = HD ** (-0.5)
    region_mask = window_mask(region_label)
    inverse_order = jnp.zeros((RES * RES,), jnp.int32).at[roll_order].set(jnp.arange(RES * RES, dtype=jnp.int32))
    flat_index = offset_index.reshape(-1)

    def one_group(carry, inputs):
        token_rows, grad_rows = inputs
        residual = token_rows.astype(jnp.float32)
        records = []
        for layer_index in range(LAYERS):
            shifted = layer_index % 2 == 1
            normed, unit_one, scale_one = normalize(residual, norm_gain[layer_index, 0], norm_shift[layer_index, 0])
            windowed = to_windows(normed.astype(jnp.bfloat16), images, roll_order, shifted)
            query_rows = ((matmul(windowed, input_weight[layer_index, 0]) + head_bias[layer_index, 0]) * scale).astype(jnp.bfloat16)
            key_rows = matmul(windowed, input_weight[layer_index, 1]).astype(jnp.bfloat16)
            value_rows = (matmul(windowed, input_weight[layer_index, 2]) + head_bias[layer_index, 1]).astype(jnp.bfloat16)
            offset_bias = offset_table[layer_index][offset_index].transpose(2, 0, 1)
            scores = scores_of(query_rows, key_rows, offset_bias, region_mask, shifted, images)
            row_max = lax.optimization_barrier(jnp.max(scores, axis=-1, keepdims=True))
            log_total = row_max + jnp.log(lax.optimization_barrier(jnp.sum(jnp.exp(scores - row_max), axis=-1, keepdims=True)))
            soft_low = jnp.exp(scores - log_total).astype(jnp.bfloat16)
            value_heads = value_rows.astype(jnp.float32).reshape(windows, pairs, HEADS, HD)
            context = jnp.einsum('whij,wjhd->wihd', soft_low.astype(jnp.float32), value_heads)
            context = context.astype(jnp.bfloat16).reshape(group_rows, C)
            context = from_windows(context, images, inverse_order, shifted)
            middle = residual + split_sum([context], [output_weight[layer_index]]) + output_bias[layer_index]
            normed_two, unit_two, scale_two = normalize(middle, norm_gain[layer_index, 1], norm_shift[layer_index, 1])
            normed_two = normed_two.astype(jnp.bfloat16)
            before = matmul(normed_two, expand_weight[layer_index]) + expand_bias[layer_index]
            activated, unused_slope = gelu_parts(before)
            activated = activated.astype(jnp.bfloat16)
            residual = middle + split_sum([activated], [reduce_weight[layer_index]]) + reduce_bias[layer_index]
            records.append((unit_one, scale_one, windowed, query_rows, key_rows, value_rows, offset_bias, log_total, soft_low, context, unit_two, scale_two, normed_two, before, activated))
        grad_residual = grad_rows.astype(jnp.float32)
        layer_grads = [None] * LAYERS
        for layer_index in reversed(range(LAYERS)):
            shifted = layer_index % 2 == 1
            unit_one, scale_one, windowed, query_rows, key_rows, value_rows, offset_bias, log_total, soft_low, context, unit_two, scale_two, normed_two, before, activated = records[layer_index]
            reduce_bias_part = lax.optimization_barrier(jnp.sum(grad_residual, axis=0))
            grad_low = grad_residual.astype(jnp.bfloat16)
            reduce_weight_part = matmul(activated.T, grad_low)
            unused_act, slope = gelu_parts(before)
            grad_before = matmul(grad_low, reduce_weight[layer_index].T) * slope
            grad_before_low = grad_before.astype(jnp.bfloat16)
            expand_weight_part = matmul(normed_two.T, grad_before_low)
            expand_bias_part = lax.optimization_barrier(jnp.sum(grad_before, axis=0))
            grad_normed_two = split_sum([grad_before_low], [expand_weight[layer_index].T])
            gain_two = lax.optimization_barrier(jnp.sum(grad_normed_two * unit_two, axis=0))
            shift_two = lax.optimization_barrier(jnp.sum(grad_normed_two, axis=0))
            grad_middle = grad_residual + normalize_back(grad_normed_two, unit_two, scale_two, norm_gain[layer_index, 1])
            output_bias_part = lax.optimization_barrier(jnp.sum(grad_middle, axis=0))
            grad_middle_low = grad_middle.astype(jnp.bfloat16)
            output_weight_part = matmul(context.T, grad_middle_low)
            grad_context = to_windows(matmul(grad_middle_low, output_weight[layer_index].T).astype(jnp.bfloat16), images, roll_order, shifted)
            scores = scores_of(query_rows, key_rows, offset_bias, region_mask, shifted, images)
            soft_full = jnp.exp(scores - log_total)
            context_heads = grad_context.astype(jnp.float32).reshape(windows, pairs, HEADS, HD)
            value_heads = value_rows.astype(jnp.float32).reshape(windows, pairs, HEADS, HD)
            query_heads = query_rows.astype(jnp.float32).reshape(windows, pairs, HEADS, HD)
            key_heads = key_rows.astype(jnp.float32).reshape(windows, pairs, HEADS, HD)
            grad_soft = jnp.einsum('wihd,wjhd->whij', context_heads, value_heads)
            delta = lax.optimization_barrier(jnp.sum(soft_full * grad_soft, axis=-1, keepdims=True))
            grad_scores = soft_full * (grad_soft - delta)
            bias_sums = lax.optimization_barrier(jnp.sum(grad_scores, axis=0)).reshape(HEADS, pairs * pairs).T
            table_part = jnp.zeros((NREL, HEADS), jnp.float32).at[flat_index].add(bias_sums)
            grad_scores_low = grad_scores.astype(jnp.bfloat16).astype(jnp.float32)
            grad_query = scale * jnp.einsum('whij,wjhd->wihd', grad_scores_low, key_heads).reshape(group_rows, C)
            grad_key = jnp.einsum('whij,wihd->wjhd', grad_scores_low, query_heads).reshape(group_rows, C)
            grad_value = jnp.einsum('whij,wihd->wjhd', soft_low.astype(jnp.float32), context_heads).reshape(group_rows, C)
            head_bias_part = jnp.stack([lax.optimization_barrier(jnp.sum(grad_query, axis=0)), lax.optimization_barrier(jnp.sum(grad_value, axis=0))])
            query_low = grad_query.astype(jnp.bfloat16)
            key_low = grad_key.astype(jnp.bfloat16)
            value_low = grad_value.astype(jnp.bfloat16)
            input_weight_part = jnp.stack([matmul(windowed.T, query_low), matmul(windowed.T, key_low), matmul(windowed.T, value_low)])
            grad_windowed = split_sum([query_low, key_low, value_low], [input_weight[layer_index, 0].T, input_weight[layer_index, 1].T, input_weight[layer_index, 2].T])
            grad_normed = from_windows(grad_windowed, images, inverse_order, shifted)
            gain_one = lax.optimization_barrier(jnp.sum(grad_normed * unit_one, axis=0))
            shift_one = lax.optimization_barrier(jnp.sum(grad_normed, axis=0))
            grad_residual = grad_middle + normalize_back(grad_normed, unit_one, scale_one, norm_gain[layer_index, 0])
            layer_grads[layer_index] = (jnp.stack([gain_one, gain_two]), jnp.stack([shift_one, shift_two]), input_weight_part, head_bias_part, table_part, output_weight_part, output_bias_part, expand_weight_part, expand_bias_part, reduce_weight_part, reduce_bias_part)
        stacked = tuple((jnp.stack([layer_grads[index_layer][member] for index_layer in range(LAYERS)]) for member in range(11)))
        new_carry = tuple((total + added for total, added in zip(carry, stacked)))
        return (new_carry, (residual.astype(jnp.bfloat16), grad_residual.astype(jnp.bfloat16)))
    zero_grads = (jnp.zeros((LAYERS, 2, C), jnp.float32), jnp.zeros((LAYERS, 2, C), jnp.float32), jnp.zeros((LAYERS, 3, C, C), jnp.float32), jnp.zeros((LAYERS, 2, C), jnp.float32), jnp.zeros((LAYERS, NREL, HEADS), jnp.float32), jnp.zeros((LAYERS, C, C), jnp.float32), jnp.zeros((LAYERS, C), jnp.float32), jnp.zeros((LAYERS, C, HID), jnp.float32), jnp.zeros((LAYERS, HID), jnp.float32), jnp.zeros((LAYERS, HID, C), jnp.float32), jnp.zeros((LAYERS, C), jnp.float32))
    token_groups = tokens.reshape(N_FSDP, group_rows, C)
    grad_groups = cotangent.reshape(N_FSDP, group_rows, C)
    totals, stacked_rows = lax.scan(one_group, zero_grads, (token_groups, grad_groups))
    outputs = stacked_rows[0].reshape(TOKENS, C)
    tokens_grad = stacked_rows[1].reshape(TOKENS, C)
    return (outputs, tokens_grad, totals[0], totals[1], totals[2], totals[3], totals[4], totals[5], totals[6], totals[7], totals[8], totals[9], totals[10])
```

```python
import functools

import jax
import jax.numpy as jnp
from jax import lax
from jax.experimental import pallas as pl
from jax.experimental.pallas import tpu as pltpu
from jax.sharding import PartitionSpec as P

C = 512
HEADS = 16
HD = 32
WIN = 7
RES = 14
LAYERS = 2
EPS = 1e-05
MASKED = -100.0
HIGHEST = lax.Precision.HIGHEST

CELLS = RES * RES
WTOK = WIN * WIN
SLOT = 64
WPI = (RES // WIN) ** 2
IMG_ROWS = WPI * SLOT
LANES = 128
GROUP = LANES // HD
GROUPS = HEADS // GROUP
GCOLS = GROUP * SLOT
SPAN = 208
STEP_IMAGES = 4
ROWS = STEP_IMAGES * CELLS
WROWS = STEP_IMAGES * IMG_ROWS
SWIN = STEP_IMAGES * WPI

F32 = jnp.float32
BF16 = jnp.bfloat16


def nn(x, y):
    return lax.dot_general(x, y, (((1,), (0,)), ((), ())), preferred_element_type=F32)


def nt(x, y):
    return lax.dot_general(x, y, (((1,), (1,)), ((), ())), preferred_element_type=F32)


def tn(x, y):
    return lax.dot_general(x, y, (((0,), (0,)), ((), ())), preferred_element_type=F32)


def wcols(ref, t, lo, hi):
    if len(ref.shape) == 4:
        return ref[:, t, :, lo:hi].reshape(C, hi - lo)
    return ref[t, :, lo:hi]


def split_of(ref):
    return ref.shape[1] if len(ref.shape) == 4 else ref.shape[0]


def unit_norm(values):
    center = jnp.mean(values, axis=-1, keepdims=True)
    centred = values - center
    inverse_scale = lax.rsqrt(jnp.mean(centred * centred, axis=-1, keepdims=True) + EPS)
    return centred * inverse_scale, inverse_scale


def norm_back(grad_normed, unit_rows, inverse_scale, gain):
    scaled = grad_normed * gain
    return inverse_scale * (
        scaled
        - jnp.mean(scaled, axis=-1, keepdims=True)
        - unit_rows * jnp.mean(scaled * unit_rows, axis=-1, keepdims=True)
    )


def image_span(image):
    first = image * CELLS
    start = first // 16 * 16
    return start, first - start


def to_window_matrix(order_col, image):
    start, offset = image_span(image)
    lane = lax.broadcasted_iota(jnp.int32, (IMG_ROWS, SPAN), 1)
    return jnp.where(order_col + offset == lane, 1.0, 0.0).astype(BF16)


def from_window_matrix(order_row, image):
    start, offset = image_span(image)
    row = lax.broadcasted_iota(jnp.int32, (SPAN, IMG_ROWS), 0)
    return jnp.where(order_row + offset == row, 1.0, 0.0).astype(BF16)


def spread_heads(block):
    lane = lax.broadcasted_iota(jnp.int32, block.shape, 1) // HD
    zero = jnp.zeros_like(block)
    return jnp.concatenate([jnp.where(lane == h, block, zero) for h in range(GROUP)], axis=0)


def pick_heads(stacked):
    lane = lax.broadcasted_iota(jnp.int32, (SLOT, LANES), 1) // HD
    out = stacked[0:SLOT]
    for h in range(1, GROUP):
        out = jnp.where(lane == h, stacked[h * SLOT : (h + 1) * SLOT], out)
    return out


def attn_fwd_kernel(
    h_ref, gain_ref, shift_ref, wqk_ref, wvo_ref, hb_ref, ob_ref, oc_ref, or_ref, bias_ref,
    mid_ref, aw_ref, qkv_ref, p_ref, o_ref, a_s, ow_s, ot_s, *, kinds,
):
    parts = split_of(wqk_ref)
    cw = C // parts
    unit, _ = unit_norm(h_ref[...].astype(F32))
    a_s[...] = (unit * gain_ref[...] + shift_ref[...]).astype(BF16)
    for i in range(STEP_IMAGES):
        start, _ = image_span(i)
        moved = nn(to_window_matrix(oc_ref[...], i), a_s[start : start + SPAN, :])
        aw_ref[i * IMG_ROWS : (i + 1) * IMG_ROWS, :] = moved.astype(BF16)
    a_win = aw_ref[...]
    scale = HD ** (-0.5)
    for t in range(parts):
        col = slice(t * cw, (t + 1) * cw)
        q = (nn(a_win, wcols(wqk_ref, t, 0, cw)) + hb_ref[0:1, col]) * scale
        qkv_ref[:, t * cw : (t + 1) * cw] = q.astype(BF16)
        k = nn(a_win, wcols(wqk_ref, t, cw, 2 * cw))
        qkv_ref[:, C + t * cw : C + (t + 1) * cw] = k.astype(BF16)
        v = nn(a_win, wcols(wvo_ref, t, 0, cw)) + hb_ref[1:2, col]
        qkv_ref[:, 2 * C + t * cw : 2 * C + (t + 1) * cw] = v.astype(BF16)

    def window(w, carry):
        rows = pl.ds(pl.multiple_of(w * SLOT, SLOT), SLOT)
        kind = w % kinds if kinds > 1 else 0
        for g in range(GROUPS):
            lo = g * LANES
            q = qkv_ref[rows, lo : lo + LANES]
            k = qkv_ref[rows, C + lo : C + lo + LANES]
            v = qkv_ref[rows, 2 * C + lo : 2 * C + lo + LANES]
            s = nt(k, spread_heads(q)) + bias_ref[kind, g]
            e = jnp.exp(s - jnp.max(s, axis=0, keepdims=True))
            p = (e * (1.0 / jnp.sum(e, axis=0, keepdims=True))).astype(BF16)
            p_ref[w, g] = p
            ow_s[rows, lo : lo + LANES] = pick_heads(tn(p, v)).astype(BF16)
        return carry

    lax.fori_loop(0, SWIN, window, 0, unroll=2)
    ot_s[...] = jnp.zeros_like(ot_s)
    for i in range(STEP_IMAGES):
        start, _ = image_span(i)
        part = nn(from_window_matrix(or_ref[...], i), ow_s[i * IMG_ROWS : (i + 1) * IMG_ROWS, :])
        ot_s[start : start + SPAN, :] += part
    o = ot_s[...].astype(BF16)
    o_ref[...] = o
    mid = h_ref[...].astype(F32) + ob_ref[...]
    for t in range(parts):
        mid = mid + nt(o[:, t * cw : (t + 1) * cw], wcols(wvo_ref, t, cw, 2 * cw))
    mid_ref[...] = mid


def chunk_of(ref):
    if len(ref.shape) == 4:
        return ref[:, 0].reshape(C, ref.shape[-1])
    return ref[0]


def mlp_fwd_kernel(
    mid_ref, gain_ref, shift_ref, we_ref, wr_ref, eb_ref, rb_ref,
    out_ref, c_ref, act_ref, slope_ref, total_s,
):
    step = pl.program_id(0)

    @pl.when(step == 0)
    def _():
        unit, _ = unit_norm(mid_ref[...])
        c_ref[...] = (unit * gain_ref[...] + shift_ref[...]).astype(BF16)
        total_s[...] = mid_ref[...] + rb_ref[...]

    pre = nn(c_ref[...], chunk_of(we_ref)) + eb_ref[...]
    cdf = 0.5 * (1.0 + lax.erf(pre * 0.7071067811865476))
    density = jnp.exp(-0.5 * pre * pre) * 0.3989422804014327
    act = (pre * cdf).astype(BF16)
    act_ref[...] = act
    slope_ref[...] = (cdf + pre * density).astype(BF16)
    total_s[...] += nt(act, chunk_of(wr_ref))

    @pl.when(step == pl.num_programs(0) - 1)
    def _():
        out_ref[...] = total_s[...].astype(out_ref.dtype)


def accumulate(ref, index, value, first):
    @pl.when(first)
    def _():
        ref[index] = value

    @pl.when(jnp.logical_not(first))
    def _():
        ref[index] += value


def mlp_bwd_kernel(
    g_ref, mid_ref, gain_ref, c_ref, act_ref, slope_ref, we_ref, wr_ref,
    gmid_ref, small_ref, eb_ref, grad_ref, gy_s, dc_s,
):
    step = pl.program_id(0)

    @pl.when(step == 0)
    def _():
        gy_s[...] = g_ref[...].astype(BF16)
        dc_s[...] = jnp.zeros_like(dc_s)

    gy = gy_s[...]
    dpre = nn(gy, chunk_of(wr_ref)) * slope_ref[...].astype(F32)
    dlow = dpre.astype(BF16)
    eb_ref[...] = jnp.sum(dpre, axis=0, keepdims=True)
    grad_ref[0] = tn(c_ref[...], dlow).astype(BF16)
    grad_ref[1] = tn(gy, act_ref[...]).astype(BF16)
    dc_s[...] += nt(dlow, chunk_of(we_ref))

    @pl.when(step == pl.num_programs(0) - 1)
    def _():
        g = g_ref[...].astype(F32)
        dc = dc_s[...]
        unit, inverse_scale = unit_norm(mid_ref[...])
        gmid = g + norm_back(dc, unit, inverse_scale, gain_ref[...])
        gmid_ref[...] = gmid
        small_ref[0:1, :] = jnp.sum(g, axis=0, keepdims=True)
        small_ref[1:2, :] = jnp.sum(dc * unit, axis=0, keepdims=True)
        small_ref[2:3, :] = jnp.sum(dc, axis=0, keepdims=True)
        small_ref[3:4, :] = jnp.sum(gmid, axis=0, keepdims=True)


def attn_bwd_kernel(
    part_ref, gmid_ref, h_ref, gain_ref, wqk_ref, wvo_ref, aw_ref, qkv_ref, p_ref, o_ref, oc_ref, or_ref,
    gout_ref, small_ref, table_ref, *rest,
):
    dt_s, dw_s, dqkv_s, da_s, hb_s, acc = rest[-6:]
    parts = split_of(wqk_ref)
    cw = C // parts
    step = pl.program_id(0)
    first = step == 0
    gmid = gmid_ref[...]
    gm = gmid.astype(BF16)
    for t in range(parts):
        accumulate(
            acc, (t, slice(None), slice(3 * cw, 4 * cw)), tn(gm, o_ref[:, t * cw : (t + 1) * cw]), first
        )
        dt_s[:, t * cw : (t + 1) * cw] = nn(gm, wcols(wvo_ref, t, cw, 2 * cw)).astype(BF16)
    for i in range(STEP_IMAGES):
        start, _ = image_span(i)
        moved = nn(to_window_matrix(oc_ref[...], i), dt_s[start : start + SPAN, :])
        dw_s[i * IMG_ROWS : (i + 1) * IMG_ROWS, :] = moved.astype(BF16)
    scale = HD ** (-0.5)
    hb_s[...] = jnp.zeros_like(hb_s)

    @pl.when(first)
    def _():
        table_ref[...] = jnp.zeros_like(table_ref)

    def window(w, carry):
        rows = pl.ds(pl.multiple_of(w * SLOT, SLOT), SLOT)
        for g in range(GROUPS):
            lo = g * LANES
            q = qkv_ref[rows, lo : lo + LANES]
            k = qkv_ref[rows, C + lo : C + lo + LANES]
            v = qkv_ref[rows, 2 * C + lo : 2 * C + lo + LANES]
            do_spread = spread_heads(dw_s[rows, lo : lo + LANES])
            p = p_ref[w, g]
            pf = p.astype(F32)
            dp = nt(v, do_spread)
            ds = pf * (dp - jnp.sum(pf * dp, axis=0, keepdims=True))
            table_ref[g] += ds
            dsl = ds.astype(BF16)
            dq = pick_heads(tn(dsl, k)) * scale
            dk = nn(dsl, spread_heads(q))
            dv = nn(p, do_spread)
            hb_s[0:8, lo : lo + LANES] += jnp.sum(dq.reshape(SLOT // 8, 8, LANES), axis=0)
            hb_s[8:16, lo : lo + LANES] += jnp.sum(dv.reshape(SLOT // 8, 8, LANES), axis=0)
            dqkv_s[rows, lo : lo + LANES] = dq.astype(BF16)
            dqkv_s[rows, C + lo : C + lo + LANES] = dk.astype(BF16)
            dqkv_s[rows, 2 * C + lo : 2 * C + lo + LANES] = dv.astype(BF16)
        return carry

    lax.fori_loop(0, SWIN, window, 0, unroll=2)
    a_win = aw_ref[...]
    da_win = jnp.zeros((WROWS, C), F32)
    for t in range(parts):
        dq = dqkv_s[:, t * cw : (t + 1) * cw]
        dk = dqkv_s[:, C + t * cw : C + (t + 1) * cw]
        dv = dqkv_s[:, 2 * C + t * cw : 2 * C + (t + 1) * cw]
        accumulate(acc, (t, slice(None), slice(0, cw)), tn(a_win, dq), first)
        accumulate(acc, (t, slice(None), slice(cw, 2 * cw)), tn(a_win, dk), first)
        accumulate(acc, (t, slice(None), slice(2 * cw, 3 * cw)), tn(a_win, dv), first)
        da_win = da_win + nt(dq, wcols(wqk_ref, t, 0, cw)) + nt(dk, wcols(wqk_ref, t, cw, 2 * cw))
        da_win = da_win + nt(dv, wcols(wvo_ref, t, 0, cw))
    high = da_win.astype(BF16)
    low = (da_win - high.astype(F32)).astype(BF16)
    da_s[...] = jnp.zeros_like(da_s)
    for i in range(STEP_IMAGES):
        start, _ = image_span(i)
        back = from_window_matrix(or_ref[...], i)
        rows = slice(i * IMG_ROWS, (i + 1) * IMG_ROWS)
        da_s[start : start + SPAN, :] += nn(back, high[rows]) + nn(back, low[rows])
    da = da_s[...]
    unit, inverse_scale = unit_norm(h_ref[...].astype(F32))
    gout_ref[...] = (gmid + norm_back(da, unit, inverse_scale, gain_ref[...])).astype(gout_ref.dtype)
    sums = jnp.concatenate(
        [
            jnp.sum(hb_s[0:8, :], axis=0, keepdims=True),
            jnp.sum(hb_s[8:16, :], axis=0, keepdims=True),
            jnp.sum(da * unit, axis=0, keepdims=True),
            jnp.sum(da, axis=0, keepdims=True),
        ],
        axis=0,
    )
    accumulate(small_ref, (slice(None), slice(None)), sums, first)

    @pl.when(step == pl.num_programs(0) - 1)
    def _():
        mine = part_ref[0]
        rest[0][...] = acc[mine].astype(BF16)
        if parts > 1:
            rest[1][...] = acc[1 - mine].astype(BF16)


def stepped(rows, cols):
    return pl.BlockSpec((rows, cols), lambda s: (s, 0))


def whole(shape):
    zeros = (0,) * len(shape)
    return pl.BlockSpec(shape, lambda s: zeros, pipeline_mode=pl.Buffered(1))


def result(shape):
    zeros = (0,) * len(shape)
    return pl.BlockSpec(shape, lambda s: zeros)


SMEM = pl.BlockSpec(memory_space=pltpu.SMEM)
PARAMS = pltpu.CompilerParams(vmem_limit_bytes=60 * 1024 * 1024)


def columns(weight, offset, width):
    block = weight.shape[:-1] + (width,)
    index = (0,) * (len(block) - 1) + (offset // width,)
    return pl.BlockSpec(block, lambda s: index, pipeline_mode=pl.Buffered(1))


def attention_forward(h, gain, shift, weight, head_bias, out_bias, order_col, order_row, bias):
    rows = h.shape[0]
    steps = rows // ROWS
    windows = steps * SWIN
    array, offset, width = weight
    return pl.pallas_call(
        functools.partial(attn_fwd_kernel, kinds=bias.shape[0]),
        grid=(steps,),
        in_specs=[
            stepped(ROWS, C), whole((1, C)), whole((1, C)), columns(array, offset, width),
            columns(array, offset + width, width),
            whole((2, C)), whole((1, C)), whole(order_col.shape), whole(order_row.shape), whole(bias.shape),
        ],
        out_specs=[
            stepped(ROWS, C), stepped(WROWS, C), stepped(WROWS, 3 * C),
            pl.BlockSpec((SWIN, GROUPS, SLOT, GCOLS), lambda s: (s, 0, 0, 0)), stepped(ROWS, C),
        ],
        out_shape=[
            jax.ShapeDtypeStruct((rows, C), F32),
            jax.ShapeDtypeStruct((steps * WROWS, C), BF16),
            jax.ShapeDtypeStruct((steps * WROWS, 3 * C), BF16),
            jax.ShapeDtypeStruct((windows, GROUPS, SLOT, GCOLS), BF16),
            jax.ShapeDtypeStruct((rows, C), BF16),
        ],
        scratch_shapes=[
            pltpu.VMEM((ROWS, C), BF16), pltpu.VMEM((WROWS, C), BF16), pltpu.VMEM((ROWS, C), F32),
        ],
        compiler_params=PARAMS,
        name="attn_fwd",
    )(h, gain, shift, array, array, head_bias, out_bias, order_col, order_row, bias)


def hidden_chunks(array, offset, width):
    chunk = min(512, width)
    per_part = width // chunk
    parts = array.shape[1] if len(array.shape) == 4 else array.shape[0]
    base = offset // chunk
    if len(array.shape) == 4:
        spec = pl.BlockSpec(
            (array.shape[0], 1, array.shape[2], chunk),
            lambda s: (0, s // per_part, 0, base + s % per_part),
        )
    else:
        spec = pl.BlockSpec((1, C, chunk), lambda s: (s // per_part, 0, base + s % per_part))
    return parts * per_part, chunk, spec


def mlp_forward(mid, gain, shift, weight, expand_bias, reduce_bias, out_dtype):
    rows = mid.shape[0]
    array, offset, width = weight
    hidden = expand_bias.shape[1]
    steps, chunk, expand_spec = hidden_chunks(array, offset, width)
    reduce_spec = hidden_chunks(array, offset + width, width)[2]
    across = lambda s: (0, s)
    return pl.pallas_call(
        mlp_fwd_kernel,
        grid=(steps,),
        in_specs=[
            whole((rows, C)), whole((1, C)), whole((1, C)), expand_spec, reduce_spec,
            pl.BlockSpec((1, chunk), across), whole((1, C)),
        ],
        out_specs=[
            whole((rows, C)), whole((rows, C)), pl.BlockSpec((rows, chunk), across),
            pl.BlockSpec((rows, chunk), across),
        ],
        out_shape=[
            jax.ShapeDtypeStruct((rows, C), out_dtype),
            jax.ShapeDtypeStruct((rows, C), BF16),
            jax.ShapeDtypeStruct((rows, hidden), BF16),
            jax.ShapeDtypeStruct((rows, hidden), BF16),
        ],
        scratch_shapes=[pltpu.VMEM((rows, C), F32)],
        compiler_params=PARAMS,
        name="mlp_fwd",
    )(mid, gain, shift, array, array, expand_bias, reduce_bias)


def mlp_backward(g, mid, gain, c, act, slope, weight):
    rows = g.shape[0]
    array, offset, width = weight
    hidden = act.shape[1]
    steps, chunk, expand_spec = hidden_chunks(array, offset, width)
    reduce_spec = hidden_chunks(array, offset + width, width)[2]
    across = lambda s: (0, s)
    return pl.pallas_call(
        mlp_bwd_kernel,
        grid=(steps,),
        in_specs=[
            whole((rows, C)), whole((rows, C)), whole((1, C)), whole((rows, C)),
            pl.BlockSpec((rows, chunk), across), pl.BlockSpec((rows, chunk), across),
            expand_spec, reduce_spec,
        ],
        out_specs=[
            whole((rows, C)), result((4, C)), pl.BlockSpec((1, chunk), across),
            pl.BlockSpec((2, C, chunk), lambda s: (0, 0, s)),
        ],
        out_shape=[
            jax.ShapeDtypeStruct((rows, C), F32),
            jax.ShapeDtypeStruct((4, C), F32), jax.ShapeDtypeStruct((1, hidden), F32),
            jax.ShapeDtypeStruct((2, C, hidden), BF16),
        ],
        scratch_shapes=[pltpu.VMEM((rows, C), BF16), pltpu.VMEM((rows, C), F32)],
        compiler_params=PARAMS,
        name="mlp_bwd",
    )(g, mid, gain, c, act, slope, array, array)


def attention_backward(part, gmid, h, gain, weight, a_win, qkv, probs, o, order_col, order_row, out_dtype):
    rows = gmid.shape[0]
    array, offset, width = weight
    parts = 2 * C // width
    grad_specs = [result((C, 2 * width))] * parts
    grad_shapes = [jax.ShapeDtypeStruct((C, 2 * width), BF16)] * parts
    return pl.pallas_call(
        attn_bwd_kernel,
        grid=(rows // ROWS,),
        in_specs=[
            SMEM, stepped(ROWS, C), stepped(ROWS, C), whole((1, C)), columns(array, offset, width),
            columns(array, offset + width, width),
            stepped(WROWS, C), stepped(WROWS, 3 * C),
            pl.BlockSpec((SWIN, GROUPS, SLOT, GCOLS), lambda s: (s, 0, 0, 0)), stepped(ROWS, C),
            whole(order_col.shape), whole(order_row.shape),
        ],
        out_specs=[stepped(ROWS, C), result((4, C)), result((GROUPS, SLOT, GCOLS))] + grad_specs,
        out_shape=[
            jax.ShapeDtypeStruct((rows, C), out_dtype),
            jax.ShapeDtypeStruct((4, C), F32), jax.ShapeDtypeStruct((GROUPS, SLOT, GCOLS), F32),
        ]
        + grad_shapes,
        scratch_shapes=[
            pltpu.VMEM((ROWS, C), BF16), pltpu.VMEM((WROWS, C), BF16), pltpu.VMEM((WROWS, 3 * C), BF16),
            pltpu.VMEM((ROWS, C), F32), pltpu.VMEM((16, C), F32),
            pltpu.VMEM((parts, C, 2 * width), F32),
        ],
        compiler_params=PARAMS,
        name="attn_bwd",
    )(part, gmid, h, gain, array, array, a_win, qkv, probs, o, order_col, order_row)


class Links:
    def __init__(self):
        self.fsdp = lax.axis_size("fsdp")
        self.tp = lax.axis_size("tp")
        self.bits = self.fsdp.bit_length() - 1
        self.f = lax.axis_index("fsdp")
        self.t = lax.axis_index("tp")

    def swap(self, x, axis):
        if axis == "tp":
            return lax.ppermute(x, "tp", [(i, i ^ 1) for i in range(self.tp)])
        return lax.ppermute(x, "fsdp", [(i, i ^ (1 << axis)) for i in range(self.fsdp)])

    def my_bit(self, axis):
        return self.t if axis == "tp" else (self.f >> axis) & 1

    def place(self, axis):
        return 0 if axis == "tp" else self.bits - axis

    def order(self):
        tp = ["tp"] if self.tp > 1 else []
        core = [0] if self.bits else []
        return tp + core + list(range(1, self.bits))

    def spread(self, shard):
        return shard.reshape((1,) * (self.bits + 1) + shard.shape)

    def join(self, x, other, axis):
        place = self.place(axis)
        shape = x.shape[:place] + (2,) + x.shape[place + 1 :]
        mine = lax.broadcasted_iota(jnp.int32, shape, place) == self.my_bit(axis)
        return jnp.where(mine, x, other)

    def grow(self, x, axes):
        for axis in axes:
            x = self.join(x, self.swap(x, axis), axis)
        return x

    def gathered(self, x):
        rows, cols = x.shape[-2:]
        return x.reshape(self.tp, self.fsdp * rows, cols)

    def halve(self, total, axis):
        place = self.place(axis)
        bit = self.my_bit(axis)
        keep = lax.dynamic_slice_in_dim(total, bit, 1, place)
        return keep, lax.dynamic_slice_in_dim(total, 1 - bit, 1, place)

    def rows_view(self, x):
        rows, cols = x.shape
        return x.reshape((1,) + (2,) * self.bits + (rows // self.fsdp, cols))

    def lower(self, total, axes):
        for n, axis in enumerate(axes):
            keep, send = self.halve(total.astype(BF16), axis)
            total = keep.astype(F32) + self.swap(send, axis).astype(F32)
        return total

    def reduce_tp(self, x):
        if self.tp == 1:
            return x.astype(F32)
        count, rows, cols = x.shape
        x = x.reshape(count, rows, self.tp, cols // self.tp)
        keep = lax.dynamic_slice_in_dim(x, self.t, 1, 2)
        send = lax.dynamic_slice_in_dim(x, 1 - self.t, 1, 2)
        return (keep.astype(F32) + self.swap(send, "tp").astype(F32)).reshape(count, rows, -1)

    def total(self, x):
        for axis in self.order():
            x = x + self.swap(x, axis)
        return x


def padded_pairs(offset_index):
    by_key = jnp.pad(offset_index.T, ((0, SLOT - WTOK), (0, SLOT - WTOK)), constant_values=-1)
    return by_key.reshape(1, SLOT * SLOT)


def group_layout(per_head):
    return (
        per_head.reshape(GROUPS, GROUP, SLOT, SLOT).transpose(0, 2, 1, 3).reshape(GROUPS, SLOT, GCOLS)
    )


def score_bias(table, selector):
    per_head = lax.dot_general(
        table, selector, (((0,), (0,)), ((), ())), precision=HIGHEST, preferred_element_type=F32
    )
    per_head = per_head.reshape(HEADS, SLOT, SLOT)
    key = lax.broadcasted_iota(jnp.int32, per_head.shape, 1)
    return group_layout(jnp.where(key < WTOK, per_head, jnp.float32(-1e30)))


def window_mask(region_label):
    blocks = RES // WIN
    labels = (
        region_label.reshape(blocks, WIN, blocks, WIN).transpose(0, 2, 1, 3).reshape(WPI, WTOK)
    )
    mask = jnp.where(labels[:, :, None] == labels[:, None, :], jnp.float32(0.0), jnp.float32(MASKED))
    mask = jnp.pad(mask, ((0, 0), (0, SLOT - WTOK), (0, SLOT - WTOK)))
    return jnp.tile(mask, (1, 1, GROUP))


def table_sums(sums, selector):
    per_head = sums.reshape(GROUPS, SLOT, GROUP, SLOT).transpose(0, 2, 1, 3).reshape(HEADS, SLOT * SLOT)
    return lax.dot_general(
        selector, per_head, (((1,), (1,)), ((), ())), precision=HIGHEST, preferred_element_type=F32
    )


def order_pair(order):
    slots = jnp.pad(order.reshape(WPI, WTOK), ((0, 0), (0, SLOT - WTOK)), constant_values=-10000)
    return slots.reshape(IMG_ROWS, 1), slots.reshape(1, IMG_ROWS)


def regular_order():
    blocks = RES // WIN
    cells = jnp.arange(CELLS, dtype=jnp.int32).reshape(blocks, WIN, blocks, WIN)
    return cells.transpose(0, 2, 1, 3).reshape(CELLS)


def shards(
    tokens, cotangent, norm_gain, norm_shift, input_weight, head_bias, offset_table, output_weight,
    output_bias, expand_weight, expand_bias, reduce_weight, reduce_bias, offset_index, region_label,
    roll_order,
):
    links = Links()
    parts = links.tp
    part = links.t.astype(jnp.int32).reshape(1)
    cw = input_weight.shape[3]

    shard_rows = input_weight.shape[2]
    hw = expand_weight.shape[2]
    width = 2 * cw

    def attention_shard(l):
        w = input_weight[l]
        return jnp.concatenate([w[0], w[1], w[2], output_weight[l].T], axis=1)

    def mlp_shard(l):
        return jnp.concatenate([expand_weight[l], reduce_weight[l].T], axis=1)

    later = jnp.concatenate([mlp_shard(0), attention_shard(1), mlp_shard(1)], axis=1)
    later = lax.all_gather(later, ("fsdp", "tp"), axis=0)
    later = later.reshape(links.fsdp, parts, shard_rows, later.shape[-1])
    if shard_rows % 16:
        later = later.transpose(1, 0, 2, 3).reshape(parts, C, later.shape[-1])
    near = links.gathered(links.grow(links.spread(attention_shard(0)), links.order()[::-1]))
    weights = [
        [(near, 0, width), (later, 0, hw)],
        [(later, 2 * hw, width), (later, 2 * hw + 2 * width, hw)],
    ]

    table_rows = offset_table.shape[1]
    pair_index = padded_pairs(offset_index)
    selector = (
        jnp.arange(table_rows, dtype=jnp.int32)[:, None] == pair_index
    ).astype(F32)
    mask = window_mask(region_label)
    orders = [order_pair(regular_order()), order_pair(roll_order)]
    biases = []
    for l in range(LAYERS):
        bias = score_bias(offset_table[l], selector)[None]
        if l % 2 == 1:
            bias = bias + mask[:, None]
        biases.append(bias)

    h = tokens
    saved = []
    for l in range(LAYERS):
        order_col, order_row = orders[l % 2]
        mid, a_win, qkv, probs, o = attention_forward(
            h, norm_gain[l, 0:1], norm_shift[l, 0:1], weights[l][0], head_bias[l], output_bias[l][None],
            order_col, order_row, biases[l],
        )
        out_dtype = BF16 if l == LAYERS - 1 else F32
        after, c, act, slope = mlp_forward(
            mid, norm_gain[l, 1:2], norm_shift[l, 1:2], weights[l][1], expand_bias[l][None],
            reduce_bias[l][None], out_dtype,
        )
        saved.append((h, mid, a_win, qkv, probs, o, c, act, slope))
        h = after
    outputs = h

    g = cotangent
    mlp_grads = [None] * LAYERS
    attn_parts = [None] * LAYERS
    smalls = [None] * LAYERS
    tp_axis = links.order()[0]
    for l in reversed(range(LAYERS)):
        order_col, order_row = orders[l % 2]
        h_in, mid, a_win, qkv, probs, o, c, act, slope = saved[l]
        if l == 0:
            keep, send = attn_parts[1]
            g, send = lax.optimization_barrier((g, send))
            received = links.swap(send, tp_axis)
        gmid, mlp_small, expb, mlp_grad = mlp_backward(
            g, mid, norm_gain[l, 1:2], c, act, slope, weights[l][1]
        )
        mlp_grads[l] = lax.psum_scatter(mlp_grad, "fsdp", scatter_dimension=1, tiled=True)
        if l == 0:
            gmid, received = lax.optimization_barrier((gmid, received))
            total = links.rows_view((keep.astype(F32) + received.astype(F32)).astype(BF16))
            keep, send = links.halve(total, 0)
            gmid, send, mlp_grads[1] = lax.optimization_barrier((gmid, send, mlp_grads[1]))
            received = links.swap(send, 0)
        g, attn_small, table, *attn_parts[l] = attention_backward(
            part, gmid, h_in, norm_gain[l, 0:1], weights[l][0], a_win, qkv, probs, o, order_col, order_row,
            BF16 if l == 0 else F32,
        )
        smalls[l] = (mlp_small, expb, attn_small, table_sums(table, selector))
    attn_parts[0], received = lax.optimization_barrier((attn_parts[0], received))
    upper = keep.astype(F32) + received.astype(F32)
    keep, send = attn_parts[0]
    lower = links.rows_view((keep.astype(F32) + links.swap(send, tp_axis).astype(F32)).astype(BF16))
    lower = links.lower(lower, [0])
    merged = links.lower(jnp.concatenate([lower, upper], axis=-1), list(range(1, links.bits)))
    merged = merged.reshape(shard_rows, -1)
    mlp_grads = [links.reduce_tp(x) for x in mlp_grads]
    shard_grads = [(merged[:, : 4 * cw], mlp_grads[0]), (merged[:, 4 * cw :], mlp_grads[1])]
    tokens_grad = g

    def packed(pieces):
        flat = jnp.concatenate([p.reshape(-1) for p in pieces])
        pad = -flat.size % 1024
        return jnp.pad(flat, (0, pad)).reshape(-1, 128)

    def unpacked(block, like):
        flat = block.reshape(-1)
        out = []
        at = 0
        for p in like:
            out.append(flat[at : at + p.size].reshape(p.shape))
            at += p.size
        return out

    pieces = [x for layer in smalls for x in layer]
    sums = unpacked(links.total(packed(pieces)), pieces)
    per_layer = [sums[4 * l : 4 * (l + 1)] for l in range(LAYERS)]

    gain_grad = jnp.stack([jnp.stack([s[2][2], s[0][1]]) for s in per_layer])
    shift_grad = jnp.stack([jnp.stack([s[2][3], s[0][2]]) for s in per_layer])
    head_grad = jnp.stack([s[2][0:2] for s in per_layer])
    table_grad = jnp.stack([s[3] for s in per_layer])
    outb_grad = jnp.stack([s[0][3] for s in per_layer])
    expb_grad = jnp.stack([s[1][0] for s in per_layer])
    redb_grad = jnp.stack([s[0][0] for s in per_layer])
    input_grad = jnp.stack(
        [jnp.stack([s[0][:, i * cw : (i + 1) * cw] for i in range(3)]) for s in shard_grads]
    )
    outw_grad = jnp.stack([s[0][:, 3 * cw :].T for s in shard_grads])
    expw_grad = jnp.stack([s[1][0] for s in shard_grads])
    redw_grad = jnp.stack([s[1][1].T for s in shard_grads])
    return (
        outputs, tokens_grad, gain_grad, shift_grad, input_grad, head_grad, table_grad, outw_grad,
        outb_grad, expw_grad, expb_grad, redw_grad, redb_grad,
    )


def solution(mesh):
    rows = P(("fsdp", "tp"), None)
    in_w = P(None, None, "fsdp", "tp")
    row_w = P(None, "tp", "fsdp")
    col_w = P(None, "fsdp", "tp")
    return jax.shard_map(
        shards,
        mesh=mesh,
        in_specs=(
            rows, rows, P(), P(), in_w, P(), P(), row_w, P(), col_w, P(), row_w, P(), P(), P(), P(),
        ),
        out_specs=(rows, rows, P(), P(), in_w, P(), P(), row_w, P(), col_w, P(), row_w, P()),
        check_vma=False,
    )
```

```python
import functools

import jax
import jax.numpy as jnp
from jax import lax
from jax.experimental import pallas as pl
from jax.experimental.pallas import tpu as pltpu
from jax.sharding import PartitionSpec as P

C = 512
HEADS = 16
HD = 32
WIN = 7
RES = 14
LAYERS = 2
EPS = 1e-05
MASKED = -100.0
HIGHEST = lax.Precision.HIGHEST

CELLS = RES * RES
WTOK = WIN * WIN
SLOT = 64
WPI = (RES // WIN) ** 2
IMG_ROWS = WPI * SLOT
LANES = 128
GROUP = LANES // HD
GROUPS = HEADS // GROUP
GCOLS = GROUP * SLOT
SPAN = 208
STEP_IMAGES = 4
ROWS = STEP_IMAGES * CELLS
WROWS = STEP_IMAGES * IMG_ROWS
SWIN = STEP_IMAGES * WPI

F32 = jnp.float32
BF16 = jnp.bfloat16


def nn(x, y):
    return lax.dot_general(x, y, (((1,), (0,)), ((), ())), preferred_element_type=F32)


def nt(x, y):
    return lax.dot_general(x, y, (((1,), (1,)), ((), ())), preferred_element_type=F32)


def tn(x, y):
    return lax.dot_general(x, y, (((0,), (0,)), ((), ())), preferred_element_type=F32)


def wcols(ref, t, lo, hi):
    if len(ref.shape) == 4:
        return ref[:, t, :, lo:hi].reshape(C, hi - lo)
    return ref[t, :, lo:hi]


def split_of(ref):
    return ref.shape[1] if len(ref.shape) == 4 else ref.shape[0]


def unit_norm(values):
    center = jnp.mean(values, axis=-1, keepdims=True)
    centred = values - center
    inverse_scale = lax.rsqrt(jnp.mean(centred * centred, axis=-1, keepdims=True) + EPS)
    return centred * inverse_scale, inverse_scale


def norm_back(grad_normed, unit_rows, inverse_scale, gain):
    scaled = grad_normed * gain
    return inverse_scale * (
        scaled
        - jnp.mean(scaled, axis=-1, keepdims=True)
        - unit_rows * jnp.mean(scaled * unit_rows, axis=-1, keepdims=True)
    )


def image_span(image):
    first = image * CELLS
    start = first // 16 * 16
    return start, first - start


def to_window_matrix(order_col, image):
    start, offset = image_span(image)
    lane = lax.broadcasted_iota(jnp.int32, (IMG_ROWS, SPAN), 1)
    return jnp.where(order_col + offset == lane, 1.0, 0.0).astype(BF16)


def from_window_matrix(order_row, image):
    start, offset = image_span(image)
    row = lax.broadcasted_iota(jnp.int32, (SPAN, IMG_ROWS), 0)
    return jnp.where(order_row + offset == row, 1.0, 0.0).astype(BF16)


def spread_heads(block):
    lane = lax.broadcasted_iota(jnp.int32, block.shape, 1) // HD
    zero = jnp.zeros_like(block)
    return jnp.concatenate([jnp.where(lane == h, block, zero) for h in range(GROUP)], axis=0)


def pick_heads(stacked):
    lane = lax.broadcasted_iota(jnp.int32, (SLOT, LANES), 1) // HD
    out = stacked[0:SLOT]
    for h in range(1, GROUP):
        out = jnp.where(lane == h, stacked[h * SLOT : (h + 1) * SLOT], out)
    return out


def attn_fwd_kernel(
    h_ref, gain_ref, shift_ref, wqk_ref, wvo_ref, hb_ref, ob_ref, oc_ref, or_ref, bias_ref,
    mid_ref, aw_ref, qkv_ref, p_ref, o_ref, a_s, ow_s, ot_s, *, kinds,
):
    parts = split_of(wqk_ref)
    cw = C // parts
    unit, _ = unit_norm(h_ref[...].astype(F32))
    a_s[...] = (unit * gain_ref[...] + shift_ref[...]).astype(BF16)
    for i in range(STEP_IMAGES):
        start, _ = image_span(i)
        moved = nn(to_window_matrix(oc_ref[...], i), a_s[start : start + SPAN, :])
        aw_ref[i * IMG_ROWS : (i + 1) * IMG_ROWS, :] = moved.astype(BF16)
    a_win = aw_ref[...]
    scale = HD ** (-0.5)
    for t in range(parts):
        col = slice(t * cw, (t + 1) * cw)
        q = (nn(a_win, wcols(wqk_ref, t, 0, cw)) + hb_ref[0:1, col]) * scale
        qkv_ref[:, t * cw : (t + 1) * cw] = q.astype(BF16)
        k = nn(a_win, wcols(wqk_ref, t, cw, 2 * cw))
        qkv_ref[:, C + t * cw : C + (t + 1) * cw] = k.astype(BF16)
        v = nn(a_win, wcols(wvo_ref, t, 0, cw)) + hb_ref[1:2, col]
        qkv_ref[:, 2 * C + t * cw : 2 * C + (t + 1) * cw] = v.astype(BF16)

    def window(w, carry):
        rows = pl.ds(pl.multiple_of(w * SLOT, SLOT), SLOT)
        kind = w % kinds if kinds > 1 else 0
        for g in range(GROUPS):
            lo = g * LANES
            q = qkv_ref[rows, lo : lo + LANES]
            k = qkv_ref[rows, C + lo : C + lo + LANES]
            v = qkv_ref[rows, 2 * C + lo : 2 * C + lo + LANES]
            s = nt(k, spread_heads(q)) + bias_ref[kind, g]
            e = jnp.exp(s - jnp.max(s, axis=0, keepdims=True))
            p = (e * (1.0 / jnp.sum(e, axis=0, keepdims=True))).astype(BF16)
            p_ref[w, g] = p
            ow_s[rows, lo : lo + LANES] = pick_heads(tn(p, v)).astype(BF16)
        return carry

    lax.fori_loop(0, SWIN, window, 0, unroll=4)
    ot_s[...] = jnp.zeros_like(ot_s)
    for i in range(STEP_IMAGES):
        start, _ = image_span(i)
        part = nn(from_window_matrix(or_ref[...], i), ow_s[i * IMG_ROWS : (i + 1) * IMG_ROWS, :])
        ot_s[start : start + SPAN, :] += part
    o = ot_s[...].astype(BF16)
    o_ref[...] = o
    mid = h_ref[...].astype(F32) + ob_ref[...]
    for t in range(parts):
        mid = mid + nt(o[:, t * cw : (t + 1) * cw], wcols(wvo_ref, t, cw, 2 * cw))
    mid_ref[...] = mid


def chunk_of(ref):
    if len(ref.shape) == 4:
        return ref[:, 0].reshape(C, ref.shape[-1])
    return ref[0]


def mlp_fwd_kernel(
    mid_ref, gain_ref, shift_ref, we_ref, wr_ref, eb_ref, rb_ref,
    out_ref, c_ref, act_ref, slope_ref, total_s,
):
    step = pl.program_id(0)

    @pl.when(step == 0)
    def _():
        unit, _ = unit_norm(mid_ref[...])
        c_ref[...] = (unit * gain_ref[...] + shift_ref[...]).astype(BF16)
        total_s[...] = mid_ref[...] + rb_ref[...]

    pre = nn(c_ref[...], chunk_of(we_ref)) + eb_ref[...]
    cdf = 0.5 * (1.0 + lax.erf(pre * 0.7071067811865476))
    density = jnp.exp(-0.5 * pre * pre) * 0.3989422804014327
    act = (pre * cdf).astype(BF16)
    act_ref[...] = act
    slope_ref[...] = (cdf + pre * density).astype(BF16)
    total_s[...] += nt(act, chunk_of(wr_ref))

    @pl.when(step == pl.num_programs(0) - 1)
    def _():
        out_ref[...] = total_s[...].astype(out_ref.dtype)


def accumulate(ref, index, value, first):
    @pl.when(first)
    def _():
        ref[index] = value

    @pl.when(jnp.logical_not(first))
    def _():
        ref[index] += value


def mlp_bwd_kernel(g_ref, mid_ref, gain_ref, c_ref, act_ref, slope_ref, we_ref, wr_ref, *rest):
    rider_ref = rest[0] if len(rest) > 8 else None
    gmid_ref, small_ref, eb_ref, grad_ref, gy_s, gt_s, ct_s, dc_s = rest[-8:]
    step = pl.program_id(0)

    @pl.when(step == 0)
    def _():
        gy_s[...] = g_ref[...].astype(BF16)
        gt_s[...] = gy_s[...].T
        ct_s[...] = c_ref[...].T
        dc_s[...] = jnp.zeros_like(dc_s)

    dpre = nn(gy_s[...], chunk_of(wr_ref)) * slope_ref[...].astype(F32)
    dlow = dpre.astype(BF16)
    eb_ref[...] = jnp.sum(dpre, axis=0, keepdims=True)
    grad_ref[0] = nn(ct_s[...], dlow).astype(BF16)
    grad_ref[1] = nn(gt_s[...], act_ref[...]).astype(BF16)
    if rider_ref is not None:
        grad_ref[2] = rider_ref[...]
    dc_s[...] += nt(dlow, chunk_of(we_ref))

    @pl.when(step == pl.num_programs(0) - 1)
    def _():
        g = g_ref[...].astype(F32)
        dc = dc_s[...]
        unit, inverse_scale = unit_norm(mid_ref[...])
        gmid = g + norm_back(dc, unit, inverse_scale, gain_ref[...])
        gmid_ref[...] = gmid
        small_ref[0:1, :] = jnp.sum(g, axis=0, keepdims=True)
        small_ref[1:2, :] = jnp.sum(dc * unit, axis=0, keepdims=True)
        small_ref[2:3, :] = jnp.sum(dc, axis=0, keepdims=True)
        small_ref[3:4, :] = jnp.sum(gmid, axis=0, keepdims=True)


def attn_bwd_kernel(
    gmid_ref, h_ref, gain_ref, wqk_ref, wvo_ref, aw_ref, qkv_ref, p_ref, o_ref, oc_ref, or_ref,
    gout_ref, small_ref, table_ref, grad_ref,
    dt_s, dw_s, dqkv_all, da_s, hb_s, w_s, at_s, gt_s,
):
    parts = split_of(wqk_ref)
    cw = C // parts
    step = pl.program_id(0)
    first = step == 0
    gmid = gmid_ref[...]
    gm = gmid.astype(BF16)
    gt_s[step] = gm.T
    at_s[step] = aw_ref[...].T
    dqkv_s = dqkv_all.at[step]

    @pl.when(first)
    def _():
        table_ref[...] = jnp.zeros_like(table_ref)
        for t in range(parts):
            col = t * cw
            w_s[:, col : col + cw] = wcols(wqk_ref, t, 0, cw)
            w_s[:, C + col : C + col + cw] = wcols(wqk_ref, t, cw, 2 * cw)
            w_s[:, 2 * C + col : 2 * C + col + cw] = wcols(wvo_ref, t, 0, cw)

    for t in range(parts):
        dt_s[:, t * cw : (t + 1) * cw] = nn(gm, wcols(wvo_ref, t, cw, 2 * cw)).astype(BF16)
    for i in range(STEP_IMAGES):
        start, _ = image_span(i)
        moved = nn(to_window_matrix(oc_ref[...], i), dt_s[start : start + SPAN, :])
        dw_s[i * IMG_ROWS : (i + 1) * IMG_ROWS, :] = moved.astype(BF16)
    scale = HD ** (-0.5)
    hb_s[...] = jnp.zeros_like(hb_s)

    def window(w, carry):
        rows = pl.ds(pl.multiple_of(w * SLOT, SLOT), SLOT)
        for g in range(GROUPS):
            lo = g * LANES
            q = qkv_ref[rows, lo : lo + LANES]
            k = qkv_ref[rows, C + lo : C + lo + LANES]
            v = qkv_ref[rows, 2 * C + lo : 2 * C + lo + LANES]
            do_spread = spread_heads(dw_s[rows, lo : lo + LANES])
            p = p_ref[w, g]
            pf = p.astype(F32)
            dp = nt(v, do_spread)
            ds = pf * (dp - jnp.sum(pf * dp, axis=0, keepdims=True))
            table_ref[g] += ds
            dsl = ds.astype(BF16)
            dq = pick_heads(tn(dsl, k)) * scale
            dk = nn(dsl, spread_heads(q))
            dv = nn(p, do_spread)
            hb_s[0:8, lo : lo + LANES] += jnp.sum(dq.reshape(SLOT // 8, 8, LANES), axis=0)
            hb_s[8:16, lo : lo + LANES] += jnp.sum(dv.reshape(SLOT // 8, 8, LANES), axis=0)
            dqkv_s[rows, lo : lo + LANES] = dq.astype(BF16)
            dqkv_s[rows, C + lo : C + lo + LANES] = dk.astype(BF16)
            dqkv_s[rows, 2 * C + lo : 2 * C + lo + LANES] = dv.astype(BF16)
        return carry

    lax.fori_loop(0, SWIN, window, 0, unroll=4)
    da_win = nt(dqkv_s[...], w_s[...])
    high = da_win.astype(BF16)
    low = (da_win - high.astype(F32)).astype(BF16)
    da_s[...] = jnp.zeros_like(da_s)
    for i in range(STEP_IMAGES):
        start, _ = image_span(i)
        back = from_window_matrix(or_ref[...], i)
        rows = slice(i * IMG_ROWS, (i + 1) * IMG_ROWS)
        da_s[start : start + SPAN, :] += nn(back, high[rows]) + nn(back, low[rows])
    da = da_s[...]
    unit, inverse_scale = unit_norm(h_ref[...].astype(F32))
    gout_ref[...] = (gmid + norm_back(da, unit, inverse_scale, gain_ref[...])).astype(gout_ref.dtype)
    sums = jnp.concatenate(
        [
            jnp.sum(hb_s[0:8, :], axis=0, keepdims=True),
            jnp.sum(hb_s[8:16, :], axis=0, keepdims=True),
            jnp.sum(da * unit, axis=0, keepdims=True),
            jnp.sum(da, axis=0, keepdims=True),
        ],
        axis=0,
    )
    accumulate(small_ref, (slice(None), slice(None)), sums, first)

    @pl.when(step == pl.num_programs(0) - 1)
    def _():
        steps = at_s.shape[0]
        for t in range(parts):
            for piece in range(3):
                lo = piece * C + t * cw
                value = nn(at_s[0], dqkv_all[0, :, lo : lo + cw])
                for n in range(1, steps):
                    value = value + nn(at_s[n], dqkv_all[n, :, lo : lo + cw])
                to = (4 * t + piece) * cw
                grad_ref[:, to : to + cw] = value.astype(BF16)
            value = nn(gt_s[0], o_ref[0:ROWS, t * cw : (t + 1) * cw])
            for n in range(1, steps):
                value = value + nn(gt_s[n], o_ref[n * ROWS : (n + 1) * ROWS, t * cw : (t + 1) * cw])
            to = (4 * t + 3) * cw
            grad_ref[:, to : to + cw] = value.astype(BF16)


def stepped(rows, cols):
    return pl.BlockSpec((rows, cols), lambda s: (s, 0))


def whole(shape):
    zeros = (0,) * len(shape)
    return pl.BlockSpec(shape, lambda s: zeros, pipeline_mode=pl.Buffered(1))


def result(shape):
    zeros = (0,) * len(shape)
    return pl.BlockSpec(shape, lambda s: zeros)


SMEM = pl.BlockSpec(memory_space=pltpu.SMEM)
PARAMS = pltpu.CompilerParams(vmem_limit_bytes=60 * 1024 * 1024)


def columns(weight, offset, width):
    block = weight.shape[:-1] + (width,)
    index = (0,) * (len(block) - 1) + (offset // width,)
    return pl.BlockSpec(block, lambda s: index, pipeline_mode=pl.Buffered(1))


def attention_forward(h, gain, shift, weight, head_bias, out_bias, order_col, order_row, bias):
    rows = h.shape[0]
    steps = rows // ROWS
    windows = steps * SWIN
    array, offset, width = weight
    return pl.pallas_call(
        functools.partial(attn_fwd_kernel, kinds=bias.shape[0]),
        grid=(steps,),
        in_specs=[
            stepped(ROWS, C), whole((1, C)), whole((1, C)), columns(array, offset, width),
            columns(array, offset + width, width),
            whole((2, C)), whole((1, C)), whole(order_col.shape), whole(order_row.shape), whole(bias.shape),
        ],
        out_specs=[
            stepped(ROWS, C), stepped(WROWS, C), stepped(WROWS, 3 * C),
            pl.BlockSpec((SWIN, GROUPS, SLOT, GCOLS), lambda s: (s, 0, 0, 0)), stepped(ROWS, C),
        ],
        out_shape=[
            jax.ShapeDtypeStruct((rows, C), F32),
            jax.ShapeDtypeStruct((steps * WROWS, C), BF16),
            jax.ShapeDtypeStruct((steps * WROWS, 3 * C), BF16),
            jax.ShapeDtypeStruct((windows, GROUPS, SLOT, GCOLS), BF16),
            jax.ShapeDtypeStruct((rows, C), BF16),
        ],
        scratch_shapes=[
            pltpu.VMEM((ROWS, C), BF16), pltpu.VMEM((WROWS, C), BF16), pltpu.VMEM((ROWS, C), F32),
        ],
        compiler_params=PARAMS,
        name="attn_fwd",
    )(h, gain, shift, array, array, head_bias, out_bias, order_col, order_row, bias)


def hidden_chunks(array, offset, width):
    chunk = min(512, width)
    per_part = width // chunk
    parts = array.shape[1] if len(array.shape) == 4 else array.shape[0]
    base = offset // chunk
    if len(array.shape) == 4:
        spec = pl.BlockSpec(
            (array.shape[0], 1, array.shape[2], chunk),
            lambda s: (0, s // per_part, 0, base + s % per_part),
        )
    else:
        spec = pl.BlockSpec((1, C, chunk), lambda s: (s // per_part, 0, base + s % per_part))
    return parts * per_part, chunk, spec


def mlp_forward(mid, gain, shift, weight, expand_bias, reduce_bias, out_dtype):
    rows = mid.shape[0]
    array, offset, width = weight
    hidden = expand_bias.shape[1]
    steps, chunk, expand_spec = hidden_chunks(array, offset, width)
    reduce_spec = hidden_chunks(array, offset + width, width)[2]
    across = lambda s: (0, s)
    return pl.pallas_call(
        mlp_fwd_kernel,
        grid=(steps,),
        in_specs=[
            whole((rows, C)), whole((1, C)), whole((1, C)), expand_spec, reduce_spec,
            pl.BlockSpec((1, chunk), across), whole((1, C)),
        ],
        out_specs=[
            whole((rows, C)), whole((rows, C)), pl.BlockSpec((rows, chunk), across),
            pl.BlockSpec((rows, chunk), across),
        ],
        out_shape=[
            jax.ShapeDtypeStruct((rows, C), out_dtype),
            jax.ShapeDtypeStruct((rows, C), BF16),
            jax.ShapeDtypeStruct((rows, hidden), BF16),
            jax.ShapeDtypeStruct((rows, hidden), BF16),
        ],
        scratch_shapes=[pltpu.VMEM((rows, C), F32)],
        compiler_params=PARAMS,
        name="mlp_fwd",
    )(mid, gain, shift, array, array, expand_bias, reduce_bias)


def mlp_backward(g, mid, gain, c, act, slope, weight, rider):
    rows = g.shape[0]
    array, offset, width = weight
    hidden = act.shape[1]
    steps, chunk, expand_spec = hidden_chunks(array, offset, width)
    reduce_spec = hidden_chunks(array, offset + width, width)[2]
    across = lambda s: (0, s)
    extra = [] if rider is None else [rider]
    slots = 2 + len(extra)
    return pl.pallas_call(
        mlp_bwd_kernel,
        grid=(steps,),
        in_specs=[
            whole((rows, C)), whole((rows, C)), whole((1, C)), whole((rows, C)),
            pl.BlockSpec((rows, chunk), across), pl.BlockSpec((rows, chunk), across),
            expand_spec, reduce_spec,
        ]
        + [pl.BlockSpec((C, chunk), across) for _ in extra],
        out_specs=[
            whole((rows, C)), result((4, C)), pl.BlockSpec((1, chunk), across),
            pl.BlockSpec((slots, C, chunk), lambda s: (0, 0, s)),
        ],
        out_shape=[
            jax.ShapeDtypeStruct((rows, C), F32),
            jax.ShapeDtypeStruct((4, C), F32), jax.ShapeDtypeStruct((1, hidden), F32),
            jax.ShapeDtypeStruct((slots, C, hidden), BF16),
        ],
        scratch_shapes=[
            pltpu.VMEM((rows, C), BF16), pltpu.VMEM((C, rows), BF16), pltpu.VMEM((C, rows), BF16),
            pltpu.VMEM((rows, C), F32),
        ],
        compiler_params=PARAMS,
        name="mlp_bwd",
    )(g, mid, gain, c, act, slope, array, array, *extra)


def attention_backward(gmid, h, gain, weight, a_win, qkv, probs, o, order_col, order_row, out_dtype):
    rows = gmid.shape[0]
    steps = rows // ROWS
    array, offset, width = weight
    return pl.pallas_call(
        attn_bwd_kernel,
        grid=(steps,),
        in_specs=[
            stepped(ROWS, C), stepped(ROWS, C), whole((1, C)), columns(array, offset, width),
            columns(array, offset + width, width),
            stepped(WROWS, C), stepped(WROWS, 3 * C),
            pl.BlockSpec((SWIN, GROUPS, SLOT, GCOLS), lambda s: (s, 0, 0, 0)), whole((rows, C)),
            whole(order_col.shape), whole(order_row.shape),
        ],
        out_specs=[
            stepped(ROWS, C), result((4, C)), result((GROUPS, SLOT, GCOLS)), result((C, 4 * C)),
        ],
        out_shape=[
            jax.ShapeDtypeStruct((rows, C), out_dtype),
            jax.ShapeDtypeStruct((4, C), F32), jax.ShapeDtypeStruct((GROUPS, SLOT, GCOLS), F32),
            jax.ShapeDtypeStruct((C, 4 * C), BF16),
        ],
        scratch_shapes=[
            pltpu.VMEM((ROWS, C), BF16), pltpu.VMEM((WROWS, C), BF16),
            pltpu.VMEM((steps, WROWS, 3 * C), BF16),
            pltpu.VMEM((ROWS, C), F32), pltpu.VMEM((16, C), F32), pltpu.VMEM((C, 3 * C), BF16),
            pltpu.VMEM((steps, C, WROWS), BF16), pltpu.VMEM((steps, C, ROWS), BF16),
        ],
        compiler_params=PARAMS,
        name="attn_bwd",
    )(gmid, h, gain, array, array, a_win, qkv, probs, o, order_col, order_row)


class Links:
    def __init__(self):
        self.fsdp = lax.axis_size("fsdp")
        self.tp = lax.axis_size("tp")
        self.bits = self.fsdp.bit_length() - 1
        self.f = lax.axis_index("fsdp")
        self.t = lax.axis_index("tp")

    def swap(self, x, axis):
        if axis == "tp":
            return lax.ppermute(x, "tp", [(i, i ^ 1) for i in range(self.tp)])
        return lax.ppermute(x, "fsdp", [(i, i ^ (1 << axis)) for i in range(self.fsdp)])

    def my_bit(self, axis):
        return self.t if axis == "tp" else (self.f >> axis) & 1

    def place(self, axis):
        return 0 if axis == "tp" else self.bits - axis

    def order(self):
        core = [0] if self.bits else []
        tp = ["tp"] if self.tp > 1 else []
        return core + tp + list(range(1, self.bits))

    def spread(self, shard):
        return shard.reshape((1,) * (self.bits + 1) + shard.shape)

    def join(self, x, other, axis):
        place = self.place(axis)
        shape = x.shape[:place] + (2,) + x.shape[place + 1 :]
        mine = lax.broadcasted_iota(jnp.int32, shape, place) == self.my_bit(axis)
        return jnp.where(mine, x, other)

    def grow(self, x, axes):
        for axis in axes:
            x = self.join(x, self.swap(x, axis), axis)
        return x

    def gathered(self, x):
        rows, cols = x.shape[-2:]
        return x.reshape(self.tp, self.fsdp * rows, cols)

    def halve(self, total, axis):
        if axis == "tp":
            width = total.shape[-1] // 2
            keep = lax.dynamic_slice_in_dim(total, self.t * width, width, total.ndim - 1)
            return keep, lax.dynamic_slice_in_dim(total, (1 - self.t) * width, width, total.ndim - 1)
        place = self.place(axis)
        bit = self.my_bit(axis)
        keep = lax.dynamic_slice_in_dim(total, bit, 1, place)
        return keep, lax.dynamic_slice_in_dim(total, 1 - bit, 1, place)

    def reduce(self, x):
        rows, cols = x.shape
        rows //= self.fsdp
        total = x.reshape((1,) + (2,) * self.bits + (rows, cols))
        for axis in self.order():
            keep, send = self.halve(total.astype(BF16), axis)
            total = keep.astype(F32) + self.swap(send, axis).astype(F32)
        return total.astype(F32).reshape(rows, cols // self.tp)

    def reduce_tp(self, x):
        if self.tp == 1:
            return x.astype(F32)
        count, rows, cols = x.shape
        x = x.reshape(count, rows, self.tp, cols // self.tp)
        keep = lax.dynamic_slice_in_dim(x, self.t, 1, 2)
        send = lax.dynamic_slice_in_dim(x, 1 - self.t, 1, 2)
        return (keep.astype(F32) + self.swap(send, "tp").astype(F32)).reshape(count, rows, -1)

    def total(self, x):
        for axis in self.order():
            x = x + self.swap(x, axis)
        return x


def padded_pairs(offset_index):
    by_key = jnp.pad(offset_index.T, ((0, SLOT - WTOK), (0, SLOT - WTOK)), constant_values=-1)
    return by_key.reshape(1, SLOT * SLOT)


def group_layout(per_head):
    return (
        per_head.reshape(GROUPS, GROUP, SLOT, SLOT).transpose(0, 2, 1, 3).reshape(GROUPS, SLOT, GCOLS)
    )


def score_bias(table, selector):
    per_head = lax.dot_general(
        table, selector, (((0,), (0,)), ((), ())), precision=HIGHEST, preferred_element_type=F32
    )
    per_head = per_head.reshape(HEADS, SLOT, SLOT)
    key = lax.broadcasted_iota(jnp.int32, per_head.shape, 1)
    return group_layout(jnp.where(key < WTOK, per_head, jnp.float32(-1e30)))


def window_mask(region_label):
    blocks = RES // WIN
    labels = (
        region_label.reshape(blocks, WIN, blocks, WIN).transpose(0, 2, 1, 3).reshape(WPI, WTOK)
    )
    mask = jnp.where(labels[:, :, None] == labels[:, None, :], jnp.float32(0.0), jnp.float32(MASKED))
    mask = jnp.pad(mask, ((0, 0), (0, SLOT - WTOK), (0, SLOT - WTOK)))
    return jnp.tile(mask, (1, 1, GROUP))


def table_sums(sums, selector):
    per_head = sums.reshape(GROUPS, SLOT, GROUP, SLOT).transpose(0, 2, 1, 3).reshape(HEADS, SLOT * SLOT)
    return lax.dot_general(
        selector, per_head, (((1,), (1,)), ((), ())), precision=HIGHEST, preferred_element_type=F32
    )


def order_pair(order):
    slots = jnp.pad(order.reshape(WPI, WTOK), ((0, 0), (0, SLOT - WTOK)), constant_values=-10000)
    return slots.reshape(IMG_ROWS, 1), slots.reshape(1, IMG_ROWS)


def regular_order():
    blocks = RES // WIN
    cells = jnp.arange(CELLS, dtype=jnp.int32).reshape(blocks, WIN, blocks, WIN)
    return cells.transpose(0, 2, 1, 3).reshape(CELLS)


def shards(
    tokens, cotangent, norm_gain, norm_shift, input_weight, head_bias, offset_table, output_weight,
    output_bias, expand_weight, expand_bias, reduce_weight, reduce_bias, offset_index, region_label,
    roll_order,
):
    links = Links()
    parts = links.tp
    cw = input_weight.shape[3]

    shard_rows = input_weight.shape[2]
    hw = expand_weight.shape[2]
    width = 2 * cw

    def attention_shard(l):
        w = input_weight[l]
        return jnp.concatenate([w[0], w[1], w[2], output_weight[l].T], axis=1)

    def mlp_shard(l):
        return jnp.concatenate([expand_weight[l], reduce_weight[l].T], axis=1)

    later = jnp.concatenate([mlp_shard(0), attention_shard(1), mlp_shard(1)], axis=1)
    later = lax.all_gather(later, ("fsdp", "tp"), axis=0)
    later = later.reshape(links.fsdp, parts, shard_rows, later.shape[-1])
    if shard_rows % 16:
        later = later.transpose(1, 0, 2, 3).reshape(parts, C, later.shape[-1])
    near = links.gathered(links.grow(links.spread(attention_shard(0)), links.order()[::-1]))
    weights = [
        [(near, 0, width), (later, 0, hw)],
        [(later, 2 * hw, width), (later, 2 * hw + 2 * width, hw)],
    ]

    table_rows = offset_table.shape[1]
    pair_index = padded_pairs(offset_index)
    selector = (
        jnp.arange(table_rows, dtype=jnp.int32)[:, None] == pair_index
    ).astype(F32)
    mask = window_mask(region_label)
    orders = [order_pair(regular_order()), order_pair(roll_order)]
    biases = []
    for l in range(LAYERS):
        bias = score_bias(offset_table[l], selector)[None]
        if l % 2 == 1:
            bias = bias + mask[:, None]
        biases.append(bias)

    h = tokens
    saved = []
    for l in range(LAYERS):
        order_col, order_row = orders[l % 2]
        mid, a_win, qkv, probs, o = attention_forward(
            h, norm_gain[l, 0:1], norm_shift[l, 0:1], weights[l][0], head_bias[l], output_bias[l][None],
            order_col, order_row, biases[l],
        )
        out_dtype = BF16 if l == LAYERS - 1 else F32
        after, c, act, slope = mlp_forward(
            mid, norm_gain[l, 1:2], norm_shift[l, 1:2], weights[l][1], expand_bias[l][None],
            reduce_bias[l][None], out_dtype,
        )
        saved.append((h, mid, a_win, qkv, probs, o, c, act, slope))
        h = after
    outputs = h

    g = cotangent
    mlp_grads = [None] * LAYERS
    smalls = [None] * LAYERS
    rider = None
    for l in reversed(range(LAYERS)):
        order_col, order_row = orders[l % 2]
        h_in, mid, a_win, qkv, probs, o, c, act, slope = saved[l]
        gmid, mlp_small, expb, mlp_grad = mlp_backward(
            g, mid, norm_gain[l, 1:2], c, act, slope, weights[l][1], rider
        )
        mlp_grads[l] = lax.psum_scatter(mlp_grad, "fsdp", scatter_dimension=1, tiled=True)
        if l < LAYERS - 1:
            gmid, mlp_grads[l + 1] = lax.optimization_barrier((gmid, mlp_grads[l + 1]))
        g, attn_small, table, rider = attention_backward(
            gmid, h_in, norm_gain[l, 0:1], weights[l][0], a_win, qkv, probs, o, order_col, order_row,
            BF16 if l == 0 else F32,
        )
        smalls[l] = (mlp_small, expb, attn_small, table_sums(table, selector))
    attn_grads = [links.reduce(rider)]
    mlp_grads = [links.reduce_tp(x) for x in mlp_grads]
    attn_grads += [x[2] for x in mlp_grads[:-1]]
    shard_grads = list(zip(attn_grads, mlp_grads))
    tokens_grad = g

    def packed(pieces):
        flat = jnp.concatenate([p.reshape(-1) for p in pieces])
        pad = -flat.size % 1024
        return jnp.pad(flat, (0, pad)).reshape(-1, 128)

    def unpacked(block, like):
        flat = block.reshape(-1)
        out = []
        at = 0
        for p in like:
            out.append(flat[at : at + p.size].reshape(p.shape))
            at += p.size
        return out

    pieces = [x for layer in smalls for x in layer]
    sums = unpacked(links.total(packed(pieces)), pieces)
    per_layer = [sums[4 * l : 4 * (l + 1)] for l in range(LAYERS)]

    gain_grad = jnp.stack([jnp.stack([s[2][2], s[0][1]]) for s in per_layer])
    shift_grad = jnp.stack([jnp.stack([s[2][3], s[0][2]]) for s in per_layer])
    head_grad = jnp.stack([s[2][0:2] for s in per_layer])
    table_grad = jnp.stack([s[3] for s in per_layer])
    outb_grad = jnp.stack([s[0][3] for s in per_layer])
    expb_grad = jnp.stack([s[1][0] for s in per_layer])
    redb_grad = jnp.stack([s[0][0] for s in per_layer])
    input_grad = jnp.stack(
        [jnp.stack([s[0][:, i * cw : (i + 1) * cw] for i in range(3)]) for s in shard_grads]
    )
    outw_grad = jnp.stack([s[0][:, 3 * cw :].T for s in shard_grads])
    expw_grad = jnp.stack([s[1][0] for s in shard_grads])
    redw_grad = jnp.stack([s[1][1].T for s in shard_grads])
    return (
        outputs, tokens_grad, gain_grad, shift_grad, input_grad, head_grad, table_grad, outw_grad,
        outb_grad, expw_grad, expb_grad, redw_grad, redb_grad,
    )


def solution(mesh):
    rows = P(("fsdp", "tp"), None)
    in_w = P(None, None, "fsdp", "tp")
    row_w = P(None, "tp", "fsdp")
    col_w = P(None, "fsdp", "tp")
    return jax.shard_map(
        shards,
        mesh=mesh,
        in_specs=(
            rows, rows, P(), P(), in_w, P(), P(), row_w, P(), col_w, P(), row_w, P(), P(), P(), P(),
        ),
        out_specs=(rows, rows, P(), P(), in_w, P(), P(), row_w, P(), col_w, P(), row_w, P()),
        check_vma=False,
    )
```

```python
import functools

import jax
import jax.numpy as jnp
from jax import lax
from jax.experimental import pallas as pl
from jax.experimental.pallas import tpu as pltpu
from jax.sharding import PartitionSpec as P

C = 512
HEADS = 16
HD = 32
WIN = 7
RES = 14
LAYERS = 2
EPS = 1e-05
MASKED = -100.0
HIGHEST = lax.Precision.HIGHEST

CELLS = RES * RES
WTOK = WIN * WIN
SLOT = 64
WPI = (RES // WIN) ** 2
IMG_ROWS = WPI * SLOT
LANES = 128
GROUP = LANES // HD
GROUPS = HEADS // GROUP
GCOLS = GROUP * SLOT
SPAN = 208
STEP_IMAGES = 4
ROWS = STEP_IMAGES * CELLS
WROWS = STEP_IMAGES * IMG_ROWS
SWIN = STEP_IMAGES * WPI

F32 = jnp.float32
BF16 = jnp.bfloat16


def nn(x, y):
    return lax.dot_general(x, y, (((1,), (0,)), ((), ())), preferred_element_type=F32)


def nt(x, y):
    return lax.dot_general(x, y, (((1,), (1,)), ((), ())), preferred_element_type=F32)


def tn(x, y):
    return lax.dot_general(x, y, (((0,), (0,)), ((), ())), preferred_element_type=F32)


def wcols(ref, t, lo, hi):
    if len(ref.shape) == 4:
        return ref[:, t, :, lo:hi].reshape(C, hi - lo)
    return ref[t, :, lo:hi]


def split_of(ref):
    return ref.shape[1] if len(ref.shape) == 4 else ref.shape[0]


def unit_norm(values):
    center = jnp.mean(values, axis=-1, keepdims=True)
    centred = values - center
    inverse_scale = lax.rsqrt(jnp.mean(centred * centred, axis=-1, keepdims=True) + EPS)
    return centred * inverse_scale, inverse_scale


def norm_back(grad_normed, unit_rows, inverse_scale, gain):
    scaled = grad_normed * gain
    return inverse_scale * (
        scaled
        - jnp.mean(scaled, axis=-1, keepdims=True)
        - unit_rows * jnp.mean(scaled * unit_rows, axis=-1, keepdims=True)
    )


def image_span(image):
    first = image * CELLS
    start = first // 16 * 16
    return start, first - start


def to_window_matrix(order_col, image):
    start, offset = image_span(image)
    lane = lax.broadcasted_iota(jnp.int32, (IMG_ROWS, SPAN), 1)
    return jnp.where(order_col + offset == lane, 1.0, 0.0).astype(BF16)


def from_window_matrix(order_row, image):
    start, offset = image_span(image)
    row = lax.broadcasted_iota(jnp.int32, (SPAN, IMG_ROWS), 0)
    return jnp.where(order_row + offset == row, 1.0, 0.0).astype(BF16)


def spread_heads(block):
    lane = lax.broadcasted_iota(jnp.int32, block.shape, 1) // HD
    zero = jnp.zeros_like(block)
    return jnp.concatenate([jnp.where(lane == h, block, zero) for h in range(GROUP)], axis=0)


def pick_heads(stacked):
    lane = lax.broadcasted_iota(jnp.int32, (SLOT, LANES), 1) // HD
    out = stacked[0:SLOT]
    for h in range(1, GROUP):
        out = jnp.where(lane == h, stacked[h * SLOT : (h + 1) * SLOT], out)
    return out


def attn_fwd_kernel(
    h_ref, gain_ref, shift_ref, wqk_ref, wvo_ref, hb_ref, ob_ref, oc_ref, or_ref, bias_ref,
    mid_ref, aw_ref, qkv_ref, p_ref, o_ref, a_s, ow_s, ot_s, *, kinds,
):
    parts = split_of(wqk_ref)
    cw = C // parts
    unit, _ = unit_norm(h_ref[...].astype(F32))
    a_s[...] = (unit * gain_ref[...] + shift_ref[...]).astype(BF16)
    for i in range(STEP_IMAGES):
        start, _ = image_span(i)
        moved = nn(to_window_matrix(oc_ref[...], i), a_s[start : start + SPAN, :])
        aw_ref[i * IMG_ROWS : (i + 1) * IMG_ROWS, :] = moved.astype(BF16)
    a_win = aw_ref[...]
    scale = HD ** (-0.5)
    for t in range(parts):
        col = slice(t * cw, (t + 1) * cw)
        q = (nn(a_win, wcols(wqk_ref, t, 0, cw)) + hb_ref[0:1, col]) * scale
        qkv_ref[:, t * cw : (t + 1) * cw] = q.astype(BF16)
        k = nn(a_win, wcols(wqk_ref, t, cw, 2 * cw))
        qkv_ref[:, C + t * cw : C + (t + 1) * cw] = k.astype(BF16)
        v = nn(a_win, wcols(wvo_ref, t, 0, cw)) + hb_ref[1:2, col]
        qkv_ref[:, 2 * C + t * cw : 2 * C + (t + 1) * cw] = v.astype(BF16)

    def window(w, carry):
        rows = pl.ds(pl.multiple_of(w * SLOT, SLOT), SLOT)
        kind = w % kinds if kinds > 1 else 0
        for g in range(GROUPS):
            lo = g * LANES
            q = qkv_ref[rows, lo : lo + LANES]
            k = qkv_ref[rows, C + lo : C + lo + LANES]
            v = qkv_ref[rows, 2 * C + lo : 2 * C + lo + LANES]
            s = nt(k, spread_heads(q)) + bias_ref[kind, g]
            e = jnp.exp(s - jnp.max(s, axis=0, keepdims=True))
            p = (e * (1.0 / jnp.sum(e, axis=0, keepdims=True))).astype(BF16)
            p_ref[w, g] = p
            ow_s[rows, lo : lo + LANES] = pick_heads(tn(p, v)).astype(BF16)
        return carry

    lax.fori_loop(0, SWIN, window, 0, unroll=8)
    ot_s[...] = jnp.zeros_like(ot_s)
    for i in range(STEP_IMAGES):
        start, _ = image_span(i)
        part = nn(from_window_matrix(or_ref[...], i), ow_s[i * IMG_ROWS : (i + 1) * IMG_ROWS, :])
        ot_s[start : start + SPAN, :] += part
    o = ot_s[...].astype(BF16)
    o_ref[...] = o
    mid = h_ref[...].astype(F32) + ob_ref[...]
    for t in range(parts):
        mid = mid + nt(o[:, t * cw : (t + 1) * cw], wcols(wvo_ref, t, cw, 2 * cw))
    mid_ref[...] = mid


def chunk_of(ref):
    if len(ref.shape) == 4:
        return ref[:, 0].reshape(C, ref.shape[-1])
    return ref[0]


def mlp_fwd_kernel(
    mid_ref, gain_ref, shift_ref, we_ref, wr_ref, eb_ref, rb_ref,
    out_ref, c_ref, act_ref, slope_ref, total_s,
):
    step = pl.program_id(0)

    @pl.when(step == 0)
    def _():
        unit, _ = unit_norm(mid_ref[...])
        c_ref[...] = (unit * gain_ref[...] + shift_ref[...]).astype(BF16)
        total_s[...] = mid_ref[...] + rb_ref[...]

    pre = nn(c_ref[...], chunk_of(we_ref)) + eb_ref[...]
    cdf = 0.5 * (1.0 + lax.erf(pre * 0.7071067811865476))
    density = jnp.exp(-0.5 * pre * pre) * 0.3989422804014327
    act = (pre * cdf).astype(BF16)
    act_ref[...] = act
    slope_ref[...] = (cdf + pre * density).astype(BF16)
    total_s[...] += nt(act, chunk_of(wr_ref))

    @pl.when(step == pl.num_programs(0) - 1)
    def _():
        out_ref[...] = total_s[...].astype(out_ref.dtype)


def accumulate(ref, index, value, first):
    @pl.when(first)
    def _():
        ref[index] = value

    @pl.when(jnp.logical_not(first))
    def _():
        ref[index] += value


def mlp_bwd_kernel(g_ref, mid_ref, gain_ref, c_ref, act_ref, slope_ref, we_ref, wr_ref, *rest):
    rider_ref = rest[0] if len(rest) > 8 else None
    gmid_ref, small_ref, eb_ref, grad_ref, gy_s, gt_s, ct_s, dc_s = rest[-8:]
    step = pl.program_id(0)

    @pl.when(step == 0)
    def _():
        gy_s[...] = g_ref[...].astype(BF16)
        gt_s[...] = gy_s[...].T
        ct_s[...] = c_ref[...].T
        dc_s[...] = jnp.zeros_like(dc_s)

    dpre = nn(gy_s[...], chunk_of(wr_ref)) * slope_ref[...].astype(F32)
    dlow = dpre.astype(BF16)
    eb_ref[...] = jnp.sum(dpre, axis=0, keepdims=True)
    grad_ref[0] = nn(ct_s[...], dlow).astype(BF16)
    grad_ref[1] = nn(gt_s[...], act_ref[...]).astype(BF16)
    if rider_ref is not None:
        grad_ref[2] = rider_ref[...]
    dc_s[...] += nt(dlow, chunk_of(we_ref))

    @pl.when(step == pl.num_programs(0) - 1)
    def _():
        g = g_ref[...].astype(F32)
        dc = dc_s[...]
        unit, inverse_scale = unit_norm(mid_ref[...])
        gmid = g + norm_back(dc, unit, inverse_scale, gain_ref[...])
        gmid_ref[...] = gmid
        small_ref[0:1, :] = jnp.sum(g, axis=0, keepdims=True)
        small_ref[1:2, :] = jnp.sum(dc * unit, axis=0, keepdims=True)
        small_ref[2:3, :] = jnp.sum(dc, axis=0, keepdims=True)
        small_ref[3:4, :] = jnp.sum(gmid, axis=0, keepdims=True)


def attn_bwd_kernel(
    gmid_ref, h_ref, gain_ref, wqk_ref, wvo_ref, aw_ref, qkv_ref, p_ref, o_ref, oc_ref, or_ref,
    gout_ref, small_ref, table_ref, grad_ref,
    dt_s, dw_s, dqkv_all, da_s, hb_s, w_s, at_s, gt_s,
):
    parts = split_of(wqk_ref)
    cw = C // parts
    step = pl.program_id(0)
    first = step == 0
    gmid = gmid_ref[...]
    gm = gmid.astype(BF16)
    gt_s[step] = gm.T
    at_s[step] = aw_ref[...].T
    dqkv_s = dqkv_all.at[step]

    @pl.when(first)
    def _():
        table_ref[...] = jnp.zeros_like(table_ref)
        for t in range(parts):
            col = t * cw
            w_s[:, col : col + cw] = wcols(wqk_ref, t, 0, cw)
            w_s[:, C + col : C + col + cw] = wcols(wqk_ref, t, cw, 2 * cw)
            w_s[:, 2 * C + col : 2 * C + col + cw] = wcols(wvo_ref, t, 0, cw)

    for t in range(parts):
        dt_s[:, t * cw : (t + 1) * cw] = nn(gm, wcols(wvo_ref, t, cw, 2 * cw)).astype(BF16)
    for i in range(STEP_IMAGES):
        start, _ = image_span(i)
        moved = nn(to_window_matrix(oc_ref[...], i), dt_s[start : start + SPAN, :])
        dw_s[i * IMG_ROWS : (i + 1) * IMG_ROWS, :] = moved.astype(BF16)
    scale = HD ** (-0.5)
    hb_s[...] = jnp.zeros_like(hb_s)

    def window(w, carry):
        rows = pl.ds(pl.multiple_of(w * SLOT, SLOT), SLOT)
        for g in range(GROUPS):
            lo = g * LANES
            q = qkv_ref[rows, lo : lo + LANES]
            k = qkv_ref[rows, C + lo : C + lo + LANES]
            v = qkv_ref[rows, 2 * C + lo : 2 * C + lo + LANES]
            do_spread = spread_heads(dw_s[rows, lo : lo + LANES])
            p = p_ref[w, g]
            pf = p.astype(F32)
            dp = nt(v, do_spread)
            ds = pf * (dp - jnp.sum(pf * dp, axis=0, keepdims=True))
            table_ref[g] += ds
            dsl = ds.astype(BF16)
            dq = pick_heads(tn(dsl, k)) * scale
            dk = nn(dsl, spread_heads(q))
            dv = nn(p, do_spread)
            hb_s[0:8, lo : lo + LANES] += jnp.sum(dq.reshape(SLOT // 8, 8, LANES), axis=0)
            hb_s[8:16, lo : lo + LANES] += jnp.sum(dv.reshape(SLOT // 8, 8, LANES), axis=0)
            dqkv_s[rows, lo : lo + LANES] = dq.astype(BF16)
            dqkv_s[rows, C + lo : C + lo + LANES] = dk.astype(BF16)
            dqkv_s[rows, 2 * C + lo : 2 * C + lo + LANES] = dv.astype(BF16)
        return carry

    lax.fori_loop(0, SWIN, window, 0, unroll=8)
    da_win = nt(dqkv_s[...], w_s[...])
    high = da_win.astype(BF16)
    low = (da_win - high.astype(F32)).astype(BF16)
    da_s[...] = jnp.zeros_like(da_s)
    for i in range(STEP_IMAGES):
        start, _ = image_span(i)
        back = from_window_matrix(or_ref[...], i)
        rows = slice(i * IMG_ROWS, (i + 1) * IMG_ROWS)
        da_s[start : start + SPAN, :] += nn(back, high[rows]) + nn(back, low[rows])
    da = da_s[...]
    unit, inverse_scale = unit_norm(h_ref[...].astype(F32))
    gout_ref[...] = (gmid + norm_back(da, unit, inverse_scale, gain_ref[...])).astype(gout_ref.dtype)
    sums = jnp.concatenate(
        [
            jnp.sum(hb_s[0:8, :], axis=0, keepdims=True),
            jnp.sum(hb_s[8:16, :], axis=0, keepdims=True),
            jnp.sum(da * unit, axis=0, keepdims=True),
            jnp.sum(da, axis=0, keepdims=True),
        ],
        axis=0,
    )
    accumulate(small_ref, (slice(None), slice(None)), sums, first)

    @pl.when(step == pl.num_programs(0) - 1)
    def _():
        steps = at_s.shape[0]
        for t in range(parts):
            for piece in range(3):
                lo = piece * C + t * cw
                value = nn(at_s[0], dqkv_all[0, :, lo : lo + cw])
                for n in range(1, steps):
                    value = value + nn(at_s[n], dqkv_all[n, :, lo : lo + cw])
                to = (4 * t + piece) * cw
                grad_ref[:, to : to + cw] = value.astype(BF16)
            value = nn(gt_s[0], o_ref[0:ROWS, t * cw : (t + 1) * cw])
            for n in range(1, steps):
                value = value + nn(gt_s[n], o_ref[n * ROWS : (n + 1) * ROWS, t * cw : (t + 1) * cw])
            to = (4 * t + 3) * cw
            grad_ref[:, to : to + cw] = value.astype(BF16)


def stepped(rows, cols):
    return pl.BlockSpec((rows, cols), lambda s: (s, 0))


def whole(shape):
    zeros = (0,) * len(shape)
    return pl.BlockSpec(shape, lambda s: zeros, pipeline_mode=pl.Buffered(1))


def result(shape):
    zeros = (0,) * len(shape)
    return pl.BlockSpec(shape, lambda s: zeros)


SMEM = pl.BlockSpec(memory_space=pltpu.SMEM)
PARAMS = pltpu.CompilerParams(vmem_limit_bytes=60 * 1024 * 1024)


def columns(weight, offset, width):
    block = weight.shape[:-1] + (width,)
    index = (0,) * (len(block) - 1) + (offset // width,)
    return pl.BlockSpec(block, lambda s: index, pipeline_mode=pl.Buffered(1))


def attention_forward(h, gain, shift, weight, head_bias, out_bias, order_col, order_row, bias):
    rows = h.shape[0]
    steps = rows // ROWS
    windows = steps * SWIN
    array, offset, width = weight
    return pl.pallas_call(
        functools.partial(attn_fwd_kernel, kinds=bias.shape[0]),
        grid=(steps,),
        in_specs=[
            stepped(ROWS, C), whole((1, C)), whole((1, C)), columns(array, offset, width),
            columns(array, offset + width, width),
            whole((2, C)), whole((1, C)), whole(order_col.shape), whole(order_row.shape), whole(bias.shape),
        ],
        out_specs=[
            stepped(ROWS, C), stepped(WROWS, C), stepped(WROWS, 3 * C),
            pl.BlockSpec((SWIN, GROUPS, SLOT, GCOLS), lambda s: (s, 0, 0, 0)), stepped(ROWS, C),
        ],
        out_shape=[
            jax.ShapeDtypeStruct((rows, C), F32),
            jax.ShapeDtypeStruct((steps * WROWS, C), BF16),
            jax.ShapeDtypeStruct((steps * WROWS, 3 * C), BF16),
            jax.ShapeDtypeStruct((windows, GROUPS, SLOT, GCOLS), BF16),
            jax.ShapeDtypeStruct((rows, C), BF16),
        ],
        scratch_shapes=[
            pltpu.VMEM((ROWS, C), BF16), pltpu.VMEM((WROWS, C), BF16), pltpu.VMEM((ROWS, C), F32),
        ],
        compiler_params=PARAMS,
        name="attn_fwd",
    )(h, gain, shift, array, array, head_bias, out_bias, order_col, order_row, bias)


def hidden_chunks(array, offset, width):
    chunk = min(512, width)
    per_part = width // chunk
    parts = array.shape[1] if len(array.shape) == 4 else array.shape[0]
    base = offset // chunk
    if len(array.shape) == 4:
        spec = pl.BlockSpec(
            (array.shape[0], 1, array.shape[2], chunk),
            lambda s: (0, s // per_part, 0, base + s % per_part),
        )
    else:
        spec = pl.BlockSpec((1, C, chunk), lambda s: (s // per_part, 0, base + s % per_part))
    return parts * per_part, chunk, spec


def mlp_forward(mid, gain, shift, weight, expand_bias, reduce_bias, out_dtype):
    rows = mid.shape[0]
    array, offset, width = weight
    hidden = expand_bias.shape[1]
    steps, chunk, expand_spec = hidden_chunks(array, offset, width)
    reduce_spec = hidden_chunks(array, offset + width, width)[2]
    across = lambda s: (0, s)
    return pl.pallas_call(
        mlp_fwd_kernel,
        grid=(steps,),
        in_specs=[
            whole((rows, C)), whole((1, C)), whole((1, C)), expand_spec, reduce_spec,
            pl.BlockSpec((1, chunk), across), whole((1, C)),
        ],
        out_specs=[
            whole((rows, C)), whole((rows, C)), pl.BlockSpec((rows, chunk), across),
            pl.BlockSpec((rows, chunk), across),
        ],
        out_shape=[
            jax.ShapeDtypeStruct((rows, C), out_dtype),
            jax.ShapeDtypeStruct((rows, C), BF16),
            jax.ShapeDtypeStruct((rows, hidden), BF16),
            jax.ShapeDtypeStruct((rows, hidden), BF16),
        ],
        scratch_shapes=[pltpu.VMEM((rows, C), F32)],
        compiler_params=PARAMS,
        name="mlp_fwd",
    )(mid, gain, shift, array, array, expand_bias, reduce_bias)


def mlp_backward(g, mid, gain, c, act, slope, weight, rider):
    rows = g.shape[0]
    array, offset, width = weight
    hidden = act.shape[1]
    steps, chunk, expand_spec = hidden_chunks(array, offset, width)
    reduce_spec = hidden_chunks(array, offset + width, width)[2]
    across = lambda s: (0, s)
    extra = [] if rider is None else [rider]
    slots = 2 + len(extra)
    return pl.pallas_call(
        mlp_bwd_kernel,
        grid=(steps,),
        in_specs=[
            whole((rows, C)), whole((rows, C)), whole((1, C)), whole((rows, C)),
            pl.BlockSpec((rows, chunk), across), pl.BlockSpec((rows, chunk), across),
            expand_spec, reduce_spec,
        ]
        + [pl.BlockSpec((C, chunk), across) for _ in extra],
        out_specs=[
            whole((rows, C)), result((4, C)), pl.BlockSpec((1, chunk), across),
            pl.BlockSpec((slots, C, chunk), lambda s: (0, 0, s)),
        ],
        out_shape=[
            jax.ShapeDtypeStruct((rows, C), F32),
            jax.ShapeDtypeStruct((4, C), F32), jax.ShapeDtypeStruct((1, hidden), F32),
            jax.ShapeDtypeStruct((slots, C, hidden), BF16),
        ],
        scratch_shapes=[
            pltpu.VMEM((rows, C), BF16), pltpu.VMEM((C, rows), BF16), pltpu.VMEM((C, rows), BF16),
            pltpu.VMEM((rows, C), F32),
        ],
        compiler_params=PARAMS,
        name="mlp_bwd",
    )(g, mid, gain, c, act, slope, array, array, *extra)


def attention_backward(gmid, h, gain, weight, a_win, qkv, probs, o, order_col, order_row, out_dtype):
    rows = gmid.shape[0]
    steps = rows // ROWS
    array, offset, width = weight
    return pl.pallas_call(
        attn_bwd_kernel,
        grid=(steps,),
        in_specs=[
            stepped(ROWS, C), stepped(ROWS, C), whole((1, C)), columns(array, offset, width),
            columns(array, offset + width, width),
            stepped(WROWS, C), stepped(WROWS, 3 * C),
            pl.BlockSpec((SWIN, GROUPS, SLOT, GCOLS), lambda s: (s, 0, 0, 0)), whole((rows, C)),
            whole(order_col.shape), whole(order_row.shape),
        ],
        out_specs=[
            stepped(ROWS, C), result((4, C)), result((GROUPS, SLOT, GCOLS)), result((C, 4 * C)),
        ],
        out_shape=[
            jax.ShapeDtypeStruct((rows, C), out_dtype),
            jax.ShapeDtypeStruct((4, C), F32), jax.ShapeDtypeStruct((GROUPS, SLOT, GCOLS), F32),
            jax.ShapeDtypeStruct((C, 4 * C), BF16),
        ],
        scratch_shapes=[
            pltpu.VMEM((ROWS, C), BF16), pltpu.VMEM((WROWS, C), BF16),
            pltpu.VMEM((steps, WROWS, 3 * C), BF16),
            pltpu.VMEM((ROWS, C), F32), pltpu.VMEM((16, C), F32), pltpu.VMEM((C, 3 * C), BF16),
            pltpu.VMEM((steps, C, WROWS), BF16), pltpu.VMEM((steps, C, ROWS), BF16),
        ],
        compiler_params=PARAMS,
        name="attn_bwd",
    )(gmid, h, gain, array, array, a_win, qkv, probs, o, order_col, order_row)


class Links:
    def __init__(self):
        self.fsdp = lax.axis_size("fsdp")
        self.tp = lax.axis_size("tp")
        self.bits = self.fsdp.bit_length() - 1
        self.f = lax.axis_index("fsdp")
        self.t = lax.axis_index("tp")

    def swap(self, x, axis):
        if axis == "tp":
            return lax.ppermute(x, "tp", [(i, i ^ 1) for i in range(self.tp)])
        return lax.ppermute(x, "fsdp", [(i, i ^ (1 << axis)) for i in range(self.fsdp)])

    def my_bit(self, axis):
        return self.t if axis == "tp" else (self.f >> axis) & 1

    def place(self, axis):
        return 0 if axis == "tp" else self.bits - axis

    def order(self):
        core = [0] if self.bits else []
        tp = ["tp"] if self.tp > 1 else []
        return core + tp + list(range(1, self.bits))

    def spread(self, shard):
        return shard.reshape((1,) * (self.bits + 1) + shard.shape)

    def join(self, x, other, axis):
        place = self.place(axis)
        shape = x.shape[:place] + (2,) + x.shape[place + 1 :]
        mine = lax.broadcasted_iota(jnp.int32, shape, place) == self.my_bit(axis)
        return jnp.where(mine, x, other)

    def grow(self, x, axes):
        for axis in axes:
            x = self.join(x, self.swap(x, axis), axis)
        return x

    def gathered(self, x):
        rows, cols = x.shape[-2:]
        return x.reshape(self.tp, self.fsdp * rows, cols)

    def halve(self, total, axis):
        if axis == "tp":
            width = total.shape[-1] // 2
            keep = lax.dynamic_slice_in_dim(total, self.t * width, width, total.ndim - 1)
            return keep, lax.dynamic_slice_in_dim(total, (1 - self.t) * width, width, total.ndim - 1)
        place = self.place(axis)
        bit = self.my_bit(axis)
        keep = lax.dynamic_slice_in_dim(total, bit, 1, place)
        return keep, lax.dynamic_slice_in_dim(total, 1 - bit, 1, place)

    def reduce(self, x, vector, late):
        rows, cols = x.shape
        rows //= self.fsdp
        total = x.reshape((1,) + (2,) * self.bits + (rows, cols))
        axes = self.order()
        for n, axis in enumerate(axes):
            keep, send = self.halve(total.astype(BF16), axis)
            if n:
                send, vector = lax.optimization_barrier((send, vector))
            received = self.swap(send, axis)
            if n:
                other = self.swap(vector, axes[n - 1])
                received, other = lax.optimization_barrier((received, other))
                vector = vector + other
            total = keep.astype(F32) + received.astype(F32)
        vector, late = lax.optimization_barrier((vector, late))
        late = [self.reduce_tp(x) for x in late]
        if axes:
            vector = vector + self.swap(vector, axes[-1])
        return total.astype(F32).reshape(rows, cols // self.tp), vector, late

    def reduce_tp(self, x):
        if self.tp == 1:
            return x.astype(F32)
        count, rows, cols = x.shape
        x = x.reshape(count, rows, self.tp, cols // self.tp)
        keep = lax.dynamic_slice_in_dim(x, self.t, 1, 2)
        send = lax.dynamic_slice_in_dim(x, 1 - self.t, 1, 2)
        return (keep.astype(F32) + self.swap(send, "tp").astype(F32)).reshape(count, rows, -1)


def padded_pairs(offset_index):
    by_key = jnp.pad(offset_index.T, ((0, SLOT - WTOK), (0, SLOT - WTOK)), constant_values=-1)
    return by_key.reshape(1, SLOT * SLOT)


def group_layout(per_head):
    return (
        per_head.reshape(GROUPS, GROUP, SLOT, SLOT).transpose(0, 2, 1, 3).reshape(GROUPS, SLOT, GCOLS)
    )


def score_bias(table, selector):
    per_head = lax.dot_general(
        table, selector, (((0,), (0,)), ((), ())), precision=HIGHEST, preferred_element_type=F32
    )
    per_head = per_head.reshape(HEADS, SLOT, SLOT)
    key = lax.broadcasted_iota(jnp.int32, per_head.shape, 1)
    return group_layout(jnp.where(key < WTOK, per_head, jnp.float32(-1e30)))


def window_mask(region_label):
    blocks = RES // WIN
    labels = (
        region_label.reshape(blocks, WIN, blocks, WIN).transpose(0, 2, 1, 3).reshape(WPI, WTOK)
    )
    mask = jnp.where(labels[:, :, None] == labels[:, None, :], jnp.float32(0.0), jnp.float32(MASKED))
    mask = jnp.pad(mask, ((0, 0), (0, SLOT - WTOK), (0, SLOT - WTOK)))
    return jnp.tile(mask, (1, 1, GROUP))


def table_sums(sums, selector):
    per_head = sums.reshape(GROUPS, SLOT, GROUP, SLOT).transpose(0, 2, 1, 3).reshape(HEADS, SLOT * SLOT)
    return lax.dot_general(
        selector, per_head, (((1,), (1,)), ((), ())), precision=HIGHEST, preferred_element_type=F32
    )


def order_pair(order):
    slots = jnp.pad(order.reshape(WPI, WTOK), ((0, 0), (0, SLOT - WTOK)), constant_values=-10000)
    return slots.reshape(IMG_ROWS, 1), slots.reshape(1, IMG_ROWS)


def regular_order():
    blocks = RES // WIN
    cells = jnp.arange(CELLS, dtype=jnp.int32).reshape(blocks, WIN, blocks, WIN)
    return cells.transpose(0, 2, 1, 3).reshape(CELLS)


def shards(
    tokens, cotangent, norm_gain, norm_shift, input_weight, head_bias, offset_table, output_weight,
    output_bias, expand_weight, expand_bias, reduce_weight, reduce_bias, offset_index, region_label,
    roll_order,
):
    links = Links()
    parts = links.tp
    cw = input_weight.shape[3]

    shard_rows = input_weight.shape[2]
    hw = expand_weight.shape[2]
    width = 2 * cw

    def attention_shard(l):
        w = input_weight[l]
        return jnp.concatenate([w[0], w[1], w[2], output_weight[l].T], axis=1)

    def mlp_shard(l):
        return jnp.concatenate([expand_weight[l], reduce_weight[l].T], axis=1)

    later = jnp.concatenate([mlp_shard(0), attention_shard(1), mlp_shard(1)], axis=1)
    later = lax.all_gather(later, ("fsdp", "tp"), axis=0)
    later = later.reshape(links.fsdp, parts, shard_rows, later.shape[-1])
    if shard_rows % 16:
        later = later.transpose(1, 0, 2, 3).reshape(parts, C, later.shape[-1])
    near = links.gathered(links.grow(links.spread(attention_shard(0)), links.order()[::-1]))
    weights = [
        [(near, 0, width), (later, 0, hw)],
        [(later, 2 * hw, width), (later, 2 * hw + 2 * width, hw)],
    ]

    table_rows = offset_table.shape[1]
    pair_index = padded_pairs(offset_index)
    selector = (
        jnp.arange(table_rows, dtype=jnp.int32)[:, None] == pair_index
    ).astype(F32)
    mask = window_mask(region_label)
    orders = [order_pair(regular_order()), order_pair(roll_order)]
    biases = []
    for l in range(LAYERS):
        bias = score_bias(offset_table[l], selector)[None]
        if l % 2 == 1:
            bias = bias + mask[:, None]
        biases.append(bias)

    h = tokens
    saved = []
    for l in range(LAYERS):
        order_col, order_row = orders[l % 2]
        mid, a_win, qkv, probs, o = attention_forward(
            h, norm_gain[l, 0:1], norm_shift[l, 0:1], weights[l][0], head_bias[l], output_bias[l][None],
            order_col, order_row, biases[l],
        )
        out_dtype = BF16 if l == LAYERS - 1 else F32
        after, c, act, slope = mlp_forward(
            mid, norm_gain[l, 1:2], norm_shift[l, 1:2], weights[l][1], expand_bias[l][None],
            reduce_bias[l][None], out_dtype,
        )
        saved.append((h, mid, a_win, qkv, probs, o, c, act, slope))
        h = after
    outputs = h

    g = cotangent
    mlp_grads = [None] * LAYERS
    smalls = [None] * LAYERS
    rider = None
    for l in reversed(range(LAYERS)):
        order_col, order_row = orders[l % 2]
        h_in, mid, a_win, qkv, probs, o, c, act, slope = saved[l]
        gmid, mlp_small, expb, mlp_grad = mlp_backward(
            g, mid, norm_gain[l, 1:2], c, act, slope, weights[l][1], rider
        )
        mlp_grads[l] = lax.psum_scatter(mlp_grad, "fsdp", scatter_dimension=1, tiled=True)
        if l < LAYERS - 1:
            gmid, mlp_grads[l + 1] = lax.optimization_barrier((gmid, mlp_grads[l + 1]))
        g, attn_small, table, rider = attention_backward(
            gmid, h_in, norm_gain[l, 0:1], weights[l][0], a_win, qkv, probs, o, order_col, order_row,
            BF16 if l == 0 else F32,
        )
        smalls[l] = (mlp_small, expb, attn_small, table_sums(table, selector))
    tokens_grad = g

    def packed(pieces):
        flat = jnp.concatenate([p.reshape(-1) for p in pieces])
        pad = -flat.size % 1024
        return jnp.pad(flat, (0, pad)).reshape(-1, 128)

    def unpacked(block, like):
        flat = block.reshape(-1)
        out = []
        at = 0
        for p in like:
            out.append(flat[at : at + p.size].reshape(p.shape))
            at += p.size
        return out

    pieces = [x for layer in smalls for x in layer]
    last_grad, sums, mlp_grads = links.reduce(rider, packed(pieces), mlp_grads)
    attn_grads = [last_grad]
    attn_grads += [x[2] for x in mlp_grads[:-1]]
    shard_grads = list(zip(attn_grads, mlp_grads))
    sums = unpacked(sums, pieces)
    per_layer = [sums[4 * l : 4 * (l + 1)] for l in range(LAYERS)]

    gain_grad = jnp.stack([jnp.stack([s[2][2], s[0][1]]) for s in per_layer])
    shift_grad = jnp.stack([jnp.stack([s[2][3], s[0][2]]) for s in per_layer])
    head_grad = jnp.stack([s[2][0:2] for s in per_layer])
    table_grad = jnp.stack([s[3] for s in per_layer])
    outb_grad = jnp.stack([s[0][3] for s in per_layer])
    expb_grad = jnp.stack([s[1][0] for s in per_layer])
    redb_grad = jnp.stack([s[0][0] for s in per_layer])
    input_grad = jnp.stack(
        [jnp.stack([s[0][:, i * cw : (i + 1) * cw] for i in range(3)]) for s in shard_grads]
    )
    outw_grad = jnp.stack([s[0][:, 3 * cw :].T for s in shard_grads])
    expw_grad = jnp.stack([s[1][0] for s in shard_grads])
    redw_grad = jnp.stack([s[1][1].T for s in shard_grads])
    return (
        outputs, tokens_grad, gain_grad, shift_grad, input_grad, head_grad, table_grad, outw_grad,
        outb_grad, expw_grad, expb_grad, redw_grad, redb_grad,
    )


def solution(mesh):
    rows = P(("fsdp", "tp"), None)
    in_w = P(None, None, "fsdp", "tp")
    row_w = P(None, "tp", "fsdp")
    col_w = P(None, "fsdp", "tp")
    return jax.shard_map(
        shards,
        mesh=mesh,
        in_specs=(
            rows, rows, P(), P(), in_w, P(), P(), row_w, P(), col_w, P(), row_w, P(), P(), P(), P(),
        ),
        out_specs=(rows, rows, P(), P(), in_w, P(), P(), row_w, P(), col_w, P(), row_w, P()),
        check_vma=False,
    )
```
